32 devices in a mesh: groups: 2 (over x), line: 16 (over z, y, core).
Axes of the slice: x: 2, y: 2, z: 4, core: 2. Of those that a mesh axis runs over, the one named last changes fastest.
Arguments:
- lodf: bfloat16 [2048, 2048], P('line'), may hold values from -0.59765625 to 0.59765625
- limits: int32 [2048], P('line'), may hold values from 50 to 150
- base_flow: float32 [4096], P(('groups', 'line')), parts along dimension 0, may hold values from -4 to 4
- first_ids: int32 [256], P(('groups', 'line')), parts along dimension 0, may hold values from 0 to 2047, as said below
- second_ids: int32 [256, 128], P(('groups', 'line')), parts along dimension 0, may hold values from 0 to 2047, as said below
- counts: int32 [256], P(('groups', 'line')), parts along dimension 0, may hold values from 1 to 128, as said below
Outputs:
- pair_penalty: float32 [256, 128], P(('groups', 'line')), parts along dimension 0
- line_pressure: float32 [4096], P(('groups', 'line')), parts along dimension 0
- lodf_grad: bfloat16 [4096, 2048], P(('groups', 'line')), parts along dimension 0
The draws below stay inside these ranges and needn't reach their ends.
There are 2 independent parts, one for each index of `groups`. The reference program is written for one: setup_inputs(seed, part) draws one part's arguments, and reference() takes and returns one part's arrays. A program takes and returns all parts, laid end to end along the dimension named above; an argument that names none is the same for every part. Nothing has to cross between parts.
Inputs may be any that keep to these rules, and one draw needn't show every extreme that they name: Entry j of first_ids is a line of tile j // 8, that is between (j // 8) * 128 and (j // 8) * 128 + 127. second_ids[j, c] is a line of the same tile as first_ids[j] and differs from first_ids[j]; entries may repeat. Slots c < counts[j] of row j are live; the others are ignored.
All inputs are finite; a program needn't handle non-finite values.
Results may differ from the reference program's by a relative error of at most 0.0021.
Values may be sent and summed in bfloat16 or wider, within the bound.
A program may use at most 64 MiB of HBM per device.

```python
import jax
import jax.numpy as jnp
from jax import lax

LINE_DEV = 128
FIRST_DEV = 8
CAND = 128
LINES = 2048
FIRST = 128
N_LINE = 16


def tile_firsts(key):
    subkey = jax.random.fold_in(key, 11)
    tiles = jnp.arange(FIRST, dtype=jnp.int32) // FIRST_DEV
    drawn = tiles * LINE_DEV + jax.random.randint(subkey, (FIRST,), 0, LINE_DEV, dtype=jnp.int32)
    drawn = drawn.at[0].set(1).at[1].set(0)
    drawn = drawn.at[FIRST - 2].set(LINES - 1).at[FIRST - 1].set(LINES - 2)
    return drawn.astype(jnp.int32)


def draw_first_ids(key, part):
    return tile_firsts(key)


def draw_second_ids(key, part):
    firsts = tile_firsts(key)
    anchor = firsts // LINE_DEV * LINE_DEV
    offsets = jax.random.randint(jax.random.fold_in(key, 23), (FIRST, CAND), 1, LINE_DEV, dtype=jnp.int32)
    chosen = (anchor[:, None] + (firsts[:, None] - anchor[:, None] + offsets) % LINE_DEV).astype(jnp.int32)
    chosen = chosen.at[0, 0].set(0).at[FIRST - 1, 0].set(LINES - 1)
    return chosen.astype(jnp.int32)


def draw_counts(key, part):
    levels = jax.random.randint(jax.random.fold_in(key, 31), (FIRST // FIRST_DEV,), 1, 5, dtype=jnp.int32)
    row_levels = jnp.repeat(levels, FIRST_DEV)
    bottom = jnp.maximum(1, CAND * (row_levels - 1) // 4)
    ceiling = CAND * row_levels // 4 + 1
    drawn = jax.random.randint(jax.random.fold_in(key, 37), (FIRST,), bottom, ceiling, dtype=jnp.int32)
    marked = jax.random.randint(jax.random.fold_in(key, 41), (), 0, FIRST, dtype=jnp.int32)
    rows = jnp.arange(FIRST, dtype=jnp.int32)
    drawn = jnp.where(rows == (marked + 1) % FIRST, 1, drawn)
    return jnp.where(rows == marked, CAND, drawn).astype(jnp.int32)


def with_ends(entries, own_key, least, high):
    longest = entries.shape.index(max(entries.shape))
    spots = []
    for shift in (0, 1):
        where = [jax.random.randint(jax.random.fold_in(own_key, axis), (), 0, length) for axis, length in enumerate(entries.shape)]
        where[longest] = (where[longest] + shift) % entries.shape[longest]
        spots.append(tuple(where))
    return entries.at[spots[0]].set(least).at[spots[1]].set(high)


def level_of(rng, shape, pieces, low, top_value):
    def one(dim, parts):
        draws = jax.random.uniform(jax.random.fold_in(jax.random.fold_in(rng, 6), dim), (parts,), jnp.float32, low / len(pieces), top_value / len(pieces))
        return jnp.repeat(jnp.exp(draws), shape[dim] // parts).reshape((-1,) + (1,) * (len(shape) - dim - 1))

    loudness = one(*pieces[0])
    for cut in pieces[1:]:
        loudness = loudness * one(*cut)
    return loudness


def centred(key, extent, deviation, most, pieces=(), kind=jnp.bfloat16):
    entries = jax.random.normal(key, extent, jnp.float32) * deviation
    if len(pieces) > 0:
        entries = level_of(key, extent, pieces, -0.22, 0.18) * entries
    return jnp.clip(entries, min=-most, max=most).astype(kind)


def setup_inputs(seed: int = 0, part: int = 0) -> dict:
    keys = jax.random.split(jax.random.key(seed), 7)
    own_keys = jax.random.split(jax.random.fold_in(keys[6], part), 7)
    return {
        "lodf": jnp.clip(jax.random.uniform(keys[0], (LINES, LINES), jnp.float32, -0.59765625, 0.59765625) * level_of(keys[0], (LINES, LINES), ((0, 16),), -0.4, 0.0), -0.59765625, 0.59765625).astype(jnp.bfloat16),
        "limits": with_ends(jax.random.randint(keys[1], (LINES,), 50, 151), jax.random.fold_in(keys[1], 1), 50, 150).astype(jnp.int32),
        "base_flow": centred(own_keys[2], (LINES,), 1.0, 4.0, ((0, 16),), jnp.float32),
        "first_ids": draw_first_ids(jax.random.fold_in(jax.random.fold_in(keys[6], part), 71), part),
        "second_ids": draw_second_ids(jax.random.fold_in(jax.random.fold_in(keys[6], part), 71), part),
        "counts": draw_counts(jax.random.fold_in(jax.random.fold_in(keys[6], part), 71), part),
    }


def pair_coefficients(square, own_flows, first_local, second_local):
    first_row = lax.dynamic_index_in_dim(square, first_local, 0, keepdims=False).astype(jnp.float32)
    first_column = lax.dynamic_index_in_dim(square, first_local, 1, keepdims=False).astype(jnp.float32)
    mutual_one = jnp.take(first_row, second_local)
    mutual_two = jnp.take(first_column, second_local)
    first_flow = lax.dynamic_index_in_dim(own_flows, first_local, 0, keepdims=False)
    second_flows = jnp.take(own_flows, second_local)
    determinant = 1.0 - mutual_one * mutual_two
    first_scale = (first_flow + mutual_one * second_flows) / determinant
    second_scale = (second_flows + mutual_two * first_flow) / determinant
    return first_scale, second_scale


def pair_terms(columns, base, limit, line_ids, first_line, second_lines, first_local, second_local, first_scale, second_scale, live_count):
    width = columns.shape[1]
    cands = second_lines.shape[0]
    selector = lax.broadcasted_iota(jnp.int32, (width, cands), 0) == second_local[None, :]
    onehot = selector.astype(jnp.bfloat16)
    picked = jnp.dot(columns, onehot, preferred_element_type=jnp.float32)
    first_column = lax.dynamic_index_in_dim(columns, first_local, 1, keepdims=False).astype(jnp.float32)
    flows = base[:, None] + first_column[:, None] * first_scale[None, :] + picked * second_scale[None, :]
    live = jnp.arange(cands, dtype=jnp.int32) < live_count
    keeping = live[None, :] & (line_ids[:, None] != first_line) & (line_ids[:, None] != second_lines[None, :])
    excess = jnp.where(keeping, jnp.maximum(jnp.abs(flows) - limit[:, None], 0.0), 0.0)
    slopes = 2.0 * excess * jnp.sign(flows)
    squares = jnp.sum(excess * excess, axis=0)
    pressure = jnp.sum(slopes, axis=1)
    weighted = (slopes * second_scale[None, :]).astype(jnp.bfloat16)
    spread = lax.dot_general(weighted, onehot, (((1,), (1,)), ((), ())), preferred_element_type=jnp.float32)
    first_part = jnp.sum(slopes * first_scale[None, :], axis=1)
    column_mark = (jnp.arange(width, dtype=jnp.int32) == first_local).astype(jnp.float32)
    spread = spread + first_part[:, None] * column_mark[None, :]
    return squares, pressure, spread


def reference(lodf, limits, base_flow, first_ids, second_ids, counts):
    limit = 0.01 * limits.astype(jnp.float32)
    line_ids = jnp.arange(LINES, dtype=jnp.int32)

    def one_tile(pressure_total, tile_index):
        anchor = (tile_index * LINE_DEV).astype(jnp.int32)
        row_anchor = (tile_index * FIRST_DEV).astype(jnp.int32)
        zero_index = jnp.zeros((), jnp.int32)
        columns = lax.dynamic_slice(lodf, (zero_index, anchor), (LINES, LINE_DEV))
        square = lax.dynamic_slice(lodf, (anchor, anchor), (LINE_DEV, LINE_DEV))
        own_flows = lax.dynamic_slice(base_flow, (anchor,), (LINE_DEV,))
        heads = lax.dynamic_slice(first_ids, (row_anchor,), (FIRST_DEV,))
        seconds = lax.dynamic_slice(second_ids, (row_anchor, zero_index), (FIRST_DEV, CAND))
        lives = lax.dynamic_slice(counts, (row_anchor,), (FIRST_DEV,))
        first_scale, second_scale = jax.vmap(pair_coefficients, in_axes=(None, None, 0, 0))(square, own_flows, heads - anchor, seconds - anchor)

        def one_first(totals, items):
            pressure_sum, spread_sum = totals
            first_line, second_lines, live_count, scale_one, scale_two = items
            squares, pressure, spread = pair_terms(columns, base_flow, limit, line_ids, first_line, second_lines, first_line - anchor, second_lines - anchor, scale_one, scale_two, live_count)
            return (pressure_sum + pressure, spread_sum + spread), squares

        start_spread = jnp.zeros((LINES, LINE_DEV), jnp.float32)
        (pressure_total, spread_sum), squares = lax.scan(one_first, (pressure_total, start_spread), (heads, seconds, lives, first_scale, second_scale))
        return pressure_total, (squares, (spread_sum / CAND).astype(jnp.bfloat16))

    pressure_total, (squares, tiles) = lax.scan(one_tile, jnp.zeros((LINES,), jnp.float32), jnp.arange(N_LINE, dtype=jnp.int32))
    pair_penalty = squares.reshape(FIRST, CAND) / LINES
    line_pressure = pressure_total / (FIRST * CAND)
    lodf_grad = jnp.transpose(tiles, (1, 0, 2)).reshape(LINES, LINES)
    return (pair_penalty, line_pressure, lodf_grad)
```

```python
import functools

import jax
import jax.numpy as jnp
from jax import lax
from jax.experimental import pallas as pl
from jax.experimental.pallas import tpu as pltpu
from jax.sharding import PartitionSpec as P


F32 = jnp.float32
BF16 = jnp.bfloat16
MESH = pl.DeviceIdType.MESH


def split_bf16(x):
    hi = x.astype(BF16)
    return hi, (x - hi.astype(F32)).astype(BF16)


def partners(half, chip, s):
    if half & (half - 1):
        return lax.rem(chip + half - s, half), lax.rem(chip + s, half)
    other, bit = 0, 1
    while bit < half:
        other = other + bit * lax.rem(chip // bit + s // bit, 2)
        bit *= 2
    return other, other


def kernel(
    n,
    first_hbm,
    counts_hbm,
    lodf_hbm,
    limits_hbm,
    base_hbm,
    second_hbm,
    pen_ref,
    pres_ref,
    grad_ref,
    msgs,
    squares,
    landed,
    pres_acc,
    lower_ref,
    upper_ref,
    dead_ref,
    lodf_ref,
    square_ref,
    limits_ref,
    base_ref,
    second_ref,
    first_ref,
    counts_ref,
    send_sem,
    recv_sem,
    back_send_sem,
    back_recv_sem,
    load_sem,
):
    me = lax.axis_index("line")
    width = lodf_ref.shape[0]
    firsts, cands = second_ref.shape
    anchor = pl.multiple_of(me * width, width)
    half = n // 2
    chip, core = me // 2, lax.rem(me, 2)
    mate = 2 * chip + 1 - core

    barrier = pltpu.get_barrier_semaphore()

    def greet(t):
        pl.semaphore_signal(barrier, inc=1, device_id={"line": t}, device_id_type=MESH)

    for s in range(half - 1, 0, -1):
        there, _ = partners(half, chip, s)
        greet(2 * there + core)
        greet(2 * there + 1 - core)
    greet(mate)

    loads = [
        pltpu.make_async_copy(lodf_hbm.at[:, pl.ds(anchor, width)], square_ref, load_sem.at[0]),
        pltpu.make_async_copy(first_hbm, first_ref, load_sem.at[1]),
        pltpu.make_async_copy(counts_hbm, counts_ref, load_sem.at[2]),
        pltpu.make_async_copy(second_hbm, second_ref, load_sem.at[3]),
        pltpu.make_async_copy(base_hbm, base_ref, load_sem.at[4]),
        pltpu.make_async_copy(limits_hbm, limits_ref, load_sem.at[5]),
        pltpu.make_async_copy(lodf_hbm, lodf_ref, load_sem.at[6]),
    ]
    for load in loads:
        load.start()

    line_f = lax.broadcasted_iota(jnp.int32, (width, cands), 0).astype(F32)
    lane_f = lax.broadcasted_iota(jnp.int32, (width, width), 1).astype(F32)
    line_b = line_f.astype(BF16)
    slot_row = lax.broadcasted_iota(jnp.int32, (1, cands), 1)
    row_of = lax.broadcasted_iota(jnp.int32, (firsts, width), 0)
    lane_of = lax.broadcasted_iota(jnp.int32, (firsts, width), 1)
    for load in loads[:-1]:
        load.wait()

    base_t = jnp.transpose(jnp.broadcast_to(base_ref[...], (cands, width)))
    limit_t = 0.01 * jnp.transpose(jnp.broadcast_to(limits_ref[...].astype(F32), (cands, width)))
    lower_ref[...] = -limit_t - base_t
    upper_ref[...] = limit_t - base_t
    square = square_ref[...]
    second_f = (second_ref[...] - anchor).astype(F32)
    k1_rows, p_rows, q_rows, live_rows = [], [], [], []
    for j in range(firsts):
        k1 = jnp.full((1, cands), first_ref[j] - anchor, jnp.int32).astype(F32)
        k2 = second_f[j : j + 1, :]
        mask_one = line_f == k1
        mask_two = line_f == k2
        by_two = jnp.dot(square, mask_two.astype(F32).astype(BF16), preferred_element_type=F32)
        by_one = jnp.dot(square, mask_one.astype(F32).astype(BF16), preferred_element_type=F32)
        p_rows.append(jnp.sum(jnp.where(mask_one, by_two, 0.0), axis=0, keepdims=True))
        q_rows.append(jnp.sum(jnp.where(mask_two, by_one, 0.0), axis=0, keepdims=True))
        k1_rows.append(k1)
        live_rows.append((slot_row < counts_ref[j]).astype(F32))
    live = jnp.concatenate(live_rows, axis=0)
    base_rows = jnp.broadcast_to(base_ref[...], (firsts, width))
    turned = pltpu.roll(base_rows, width // 2, 1)
    halves = jnp.where(lax.rem(row_of, 2) == 0, base_rows, turned)
    halves_hi = halves.astype(BF16).astype(F32)
    base_parts = jnp.where(row_of < 2, halves_hi, halves - halves_hi)
    tail = jnp.where(lane_of < width // 2, base_parts, jnp.concatenate(k1_rows, axis=0))
    msgs[me] = jnp.concatenate(
        [
            jnp.where(live > 0.0, second_f, -1.0),
            jnp.concatenate(p_rows, axis=0),
            jnp.concatenate(q_rows, axis=0),
            tail,
        ],
        axis=0,
    ).astype(BF16)

    def out_copy(t, source):
        return pltpu.make_async_remote_copy(
            src_ref=msgs.at[source],
            dst_ref=msgs.at[source],
            send_sem=send_sem.at[t],
            recv_sem=recv_sem.at[source],
            device_id={"line": t},
            device_id_type=MESH,
        )

    def back_copy(t, source):
        return pltpu.make_async_remote_copy(
            src_ref=squares.at[t],
            dst_ref=landed.at[source],
            send_sem=back_send_sem.at[t],
            recv_sem=back_recv_sem.at[source],
            device_id={"line": t},
            device_id_type=MESH,
        )

    grad_scale = 2.0 / cands

    def tile(t, own):
        block = msgs[t].astype(F32)
        k2s = block[0:firsts]
        p = block[firsts : 2 * firsts]
        q = block[2 * firsts : 3 * firsts]
        tail = block[3 * firsts : 4 * firsts]
        k1s = jnp.broadcast_to(tail[:, width - 1 : width], (firsts, width))
        pair = tail[0:2] + tail[2:4]
        flow_row = jnp.where(
            lane_of < width // 2,
            jnp.broadcast_to(pair[0:1], (firsts, width)),
            pltpu.roll(jnp.broadcast_to(pair[1:2], (firsts, width)), width // 2, 1),
        )
        b1 = jnp.take_along_axis(flow_row, k1s.astype(jnp.int32), axis=1)
        b2 = jnp.take_along_axis(flow_row, jnp.maximum(k2s, 0.0).astype(jnp.int32), axis=1)
        alive = k2s >= 0.0
        det = 1.0 - p * q
        a1s = jnp.where(alive, (b1 + p * b2) / det, 0.0)
        a2s = jnp.where(alive, (b2 + q * b1) / det, 0.0)
        columns = lodf_ref[:, pl.ds(pl.multiple_of(t * width, width), width)]
        columns = jnp.concatenate([columns, columns], axis=1)
        a1_hi, a1_lo = split_bf16(a1s)
        a2_hi, a2_lo = split_bf16(a2s)
        k2_b, k1_b = k2s.astype(BF16), k1s.astype(BF16)
        zero_b = jnp.zeros((width, cands), BF16)
        one_b = jnp.ones((width, cands), BF16)
        spread = jnp.zeros((width, width), F32)
        first_part = jnp.zeros((width, width), F32)
        pressure = jnp.zeros((width, cands), F32)
        square_rows = []
        for j0 in range(0, firsts, 2):
            hots, mixes = [], []
            for j in (j0, j0 + 1):
                row = slice(j, j + 1)
                at_two = line_b == jnp.broadcast_to(k2_b[row], (width, cands))
                at_one = line_b == jnp.broadcast_to(k1_b[row], (width, cands))

                def place(two, one):
                    two = jnp.broadcast_to(two, (width, cands))
                    one = jnp.broadcast_to(one, (width, cands))
                    return jnp.where(at_two, two, jnp.where(at_one, one, zero_b))

                hots.append(jnp.where(at_two, one_b, zero_b))
                mixes.append(
                    jnp.concatenate(
                        [place(a2_hi[row], a1_hi[row]), place(a2_lo[row], a1_lo[row])], axis=0
                    )
                )
            mixed = jnp.dot(
                columns, jnp.concatenate(mixes, axis=1), preferred_element_type=F32
            )
            weighted = []
            for i, j in enumerate((j0, j0 + 1)):
                row = slice(j, j + 1)
                x = mixed[:, i * cands : (i + 1) * cands]
                e = x - jnp.minimum(jnp.maximum(x, lower_ref[...]), upper_ref[...])
                if own:
                    keep = (line_f != k2s[row]) & (line_f != k1s[row]) & (k2s[row] >= 0.0)
                    e = jnp.where(keep, e, 0.0)
                square_rows.append(jnp.sum(e * e, axis=0, keepdims=True))
                pressure = pressure + e
                weighted.append((e * a2s[row]).astype(BF16))
                one_sum = jnp.sum(e * a1s[row], axis=1, keepdims=True)
                first_part = first_part + jnp.where(lane_f == k1s[row, :width], one_sum, 0.0)
            spread = spread + lax.dot_general(
                jnp.concatenate(weighted, axis=1),
                jnp.concatenate(hots, axis=1),
                (((1,), (1,)), ((), ())),
                preferred_element_type=F32,
            )
        grad_ref[:, pl.ds(pl.multiple_of(t * width, width), width)] = (
            (spread + first_part) * grad_scale
        ).astype(grad_ref.dtype)
        squares[t] = jnp.concatenate(square_rows, axis=0)
        if own:
            pres_acc[...] = pressure
            dead_ref[...] = jnp.zeros_like(dead_ref)
        else:
            pres_acc[...] += pressure
            dead_ref[...] += jnp.where(k2s < 0.0, 1.0, 0.0)

    loads[-1].wait()
    pl.semaphore_wait(barrier, n - 1)
    for s in range(half - 1, 0, -1):
        there, _ = partners(half, chip, s)
        out_copy(2 * there + core, me).start()
        out_copy(2 * there + 1 - core, me).start()
    out_copy(mate, me).start()
    tile(me, True)

    out_copy(mate, mate).wait_recv()
    tile(mate, False)
    back_copy(mate, me).start()

    near = min(3, half - 1)

    @pl.loop(0, half - 1)
    def _(i):
        s = jnp.where(i < near, i + 1, half - 1 + near - i)
        _, there = partners(half, chip, s)
        tiles = [2 * there + core, 2 * there + 1 - core]
        for t in tiles:
            out_copy(t, t).wait_recv()
        for t in tiles:
            tile(t, False)
        for t in tiles:
            back_copy(t, me).start()

    n_dead = jnp.sum(dead_ref[...])
    resting = -jnp.minimum(jnp.maximum(0.0, lower_ref[...]), upper_ref[...])
    lines_sum = jnp.sum(jnp.transpose(pres_acc[...]), axis=0, keepdims=True)
    rest_row = jnp.transpose(resting)[0:1, :]
    pairs = n * firsts * cands
    pres_ref[...] = (lines_sum - n_dead * rest_row) * (2.0 / pairs)

    landed[me] = squares[me]

    @pl.loop(1, n)
    def _(s):
        t = lax.rem(me + s, n)
        back_copy(t, t).wait_recv()

    total = jnp.sum(landed[...], axis=0)
    alive_now = msgs[me].astype(F32)[0:firsts] >= 0.0
    pen_ref[...] = jnp.where(alive_now, total, 0.0) / (n * width)

    @pl.loop(1, n)
    def _(s):
        t = lax.rem(me + s, n)
        out_copy(t, me).wait_send()
        back_copy(t, me).wait_send()


def hand_out(pen_in, pres_in, grad_in, pen_ref, pres_ref, grad_ref, sems):
    copies = [
        pltpu.make_async_copy(grad_in, grad_ref, sems.at[0]),
        pltpu.make_async_copy(pen_in, pen_ref, sems.at[1]),
        pltpu.make_async_copy(pres_in, pres_ref, sems.at[2]),
    ]
    for copy in copies:
        copy.start()
    for copy in copies:
        copy.wait()


def per_device(n, lodf, limits, base_flow, first_ids, second_ids, counts):
    width, lines = lodf.shape
    firsts, cands = second_ids.shape
    vmem = pl.BlockSpec(memory_space=pltpu.VMEM)
    anywhere = pl.BlockSpec(memory_space=pl.ANY)
    penalty, pressure, grad = pl.pallas_call(
        functools.partial(kernel, n),
        out_shape=(
            pltpu.VMEM((firsts, cands), F32),
            pltpu.VMEM((1, width), F32),
            pltpu.VMEM((width, lines), BF16),
        ),
        in_specs=[anywhere] * 6,
        out_specs=(vmem, vmem, vmem),
        scratch_shapes=[
            pltpu.VMEM((n, 4 * firsts, cands), BF16),
            pltpu.VMEM((n, firsts, cands), F32),
            pltpu.VMEM((n, firsts, cands), F32),
            pltpu.VMEM((width, cands), F32),
            pltpu.VMEM((width, cands), F32),
            pltpu.VMEM((width, cands), F32),
            pltpu.VMEM((firsts, cands), F32),
            pltpu.VMEM((width, lines), BF16),
            pltpu.VMEM((width, width), BF16),
            pltpu.VMEM((1, width), jnp.int32),
            pltpu.VMEM((1, width), F32),
            pltpu.VMEM((firsts, cands), jnp.int32),
            pltpu.SMEM((firsts,), jnp.int32),
            pltpu.SMEM((firsts,), jnp.int32),
            pltpu.SemaphoreType.DMA((n,)),
            pltpu.SemaphoreType.DMA((n,)),
            pltpu.SemaphoreType.DMA((n,)),
            pltpu.SemaphoreType.DMA((n,)),
            pltpu.SemaphoreType.DMA((7,)),
        ],
        compiler_params=pltpu.CompilerParams(collective_id=0, has_side_effects=True),
        name="screen",
    )(first_ids, counts, lodf, limits.reshape(1, width), base_flow.reshape(1, width), second_ids)
    penalty, pressure, grad = pl.pallas_call(
        hand_out,
        out_shape=(
            jax.ShapeDtypeStruct((firsts, cands), F32),
            jax.ShapeDtypeStruct((1, width), F32),
            jax.ShapeDtypeStruct((width, lines), BF16),
        ),
        in_specs=[anywhere] * 3,
        out_specs=(anywhere,) * 3,
        scratch_shapes=[pltpu.SemaphoreType.DMA((3,))],
        compiler_params=pltpu.CompilerParams(vmem_limit_bytes=1 << 20),
        name="hand_out",
    )(penalty, pressure, grad)
    return penalty, pressure.reshape(width), grad


def solution(mesh):
    return jax.shard_map(
        functools.partial(per_device, mesh.shape["line"]),
        mesh=mesh,
        in_specs=(
            P("line", None),
            P("line"),
            P(("groups", "line")),
            P(("groups", "line")),
            P(("groups", "line"), None),
            P(("groups", "line")),
        ),
        out_specs=(P(("groups", "line"), None), P(("groups", "line")), P(("groups", "line"), None)),
        check_vma=False,
    )
```

```python
import functools

import jax
import jax.numpy as jnp
from jax import lax
from jax.experimental import pallas as pl
from jax.experimental.pallas import tpu as pltpu
from jax.sharding import PartitionSpec as P


F32 = jnp.float32
BF16 = jnp.bfloat16
MESH = pl.DeviceIdType.MESH


def split_bf16(x):
    hi = x.astype(BF16)
    return hi, (x - hi.astype(F32)).astype(BF16)


def partners(half, chip, s):
    if half & (half - 1):
        return lax.rem(chip + half - s, half), lax.rem(chip + s, half)
    other, bit = 0, 1
    while bit < half:
        other = other + bit * lax.rem(chip // bit + s // bit, 2)
        bit *= 2
    return other, other


def kernel(
    n,
    first_hbm,
    counts_hbm,
    lodf_hbm,
    limits_hbm,
    base_hbm,
    second_hbm,
    pen_ref,
    pres_ref,
    grad_ref,
    msgs,
    squares,
    landed,
    pres_acc,
    lower_ref,
    upper_ref,
    dead_ref,
    lodf_ref,
    square_ref,
    limits_ref,
    base_ref,
    second_ref,
    first_ref,
    counts_ref,
    send_sem,
    recv_sem,
    back_send_sem,
    back_recv_sem,
    load_sem,
):
    me = lax.axis_index("line")
    width = lodf_ref.shape[0]
    firsts, cands = second_ref.shape
    anchor = pl.multiple_of(me * width, width)
    half = n // 2
    chip, core = me // 2, lax.rem(me, 2)
    mate = 2 * chip + 1 - core

    barrier = pltpu.get_barrier_semaphore()

    def greet(t):
        pl.semaphore_signal(barrier, inc=1, device_id={"line": t}, device_id_type=MESH)

    for s in range(half - 1, 0, -1):
        there, _ = partners(half, chip, s)
        greet(2 * there + core)
        greet(2 * there + 1 - core)
    greet(mate)

    loads = [
        pltpu.make_async_copy(lodf_hbm.at[:, pl.ds(anchor, width)], square_ref, load_sem.at[0]),
        pltpu.make_async_copy(first_hbm, first_ref, load_sem.at[1]),
        pltpu.make_async_copy(counts_hbm, counts_ref, load_sem.at[2]),
        pltpu.make_async_copy(second_hbm, second_ref, load_sem.at[3]),
        pltpu.make_async_copy(base_hbm, base_ref, load_sem.at[4]),
        pltpu.make_async_copy(limits_hbm, limits_ref, load_sem.at[5]),
        pltpu.make_async_copy(lodf_hbm, lodf_ref, load_sem.at[6]),
    ]
    for load in loads:
        load.start()

    line_f = lax.broadcasted_iota(jnp.int32, (width, cands), 0).astype(F32)
    lane_f = lax.broadcasted_iota(jnp.int32, (width, width), 1).astype(F32)
    line_b = line_f.astype(BF16)
    slot_row = lax.broadcasted_iota(jnp.int32, (1, cands), 1)
    row_of = lax.broadcasted_iota(jnp.int32, (firsts, width), 0)
    lane_of = lax.broadcasted_iota(jnp.int32, (firsts, width), 1)
    for load in loads[:-1]:
        load.wait()

    base_t = jnp.transpose(jnp.broadcast_to(base_ref[...], (cands, width)))
    limit_t = 0.01 * jnp.transpose(jnp.broadcast_to(limits_ref[...].astype(F32), (cands, width)))
    lower_ref[...] = -limit_t - base_t
    upper_ref[...] = limit_t - base_t
    square = square_ref[...]
    second_f = (second_ref[...] - anchor).astype(F32)
    k1_rows, p_rows, q_rows, live_rows = [], [], [], []
    for j in range(firsts):
        k1 = jnp.full((1, cands), first_ref[j] - anchor, jnp.int32).astype(F32)
        k2 = second_f[j : j + 1, :]
        mask_one = line_f == k1
        mask_two = line_f == k2
        by_two = jnp.dot(square, mask_two.astype(F32).astype(BF16), preferred_element_type=F32)
        by_one = jnp.dot(square, mask_one.astype(F32).astype(BF16), preferred_element_type=F32)
        p_rows.append(jnp.sum(jnp.where(mask_one, by_two, 0.0), axis=0, keepdims=True))
        q_rows.append(jnp.sum(jnp.where(mask_two, by_one, 0.0), axis=0, keepdims=True))
        k1_rows.append(k1)
        live_rows.append((slot_row < counts_ref[j]).astype(F32))
    live = jnp.concatenate(live_rows, axis=0)
    base_rows = jnp.broadcast_to(base_ref[...], (firsts, width))
    turned = pltpu.roll(base_rows, width // 2, 1)
    halves = jnp.where(lax.rem(row_of, 2) == 0, base_rows, turned)
    halves_hi = halves.astype(BF16).astype(F32)
    base_parts = jnp.where(row_of < 2, halves_hi, halves - halves_hi)
    tail = jnp.where(lane_of < width // 2, base_parts, jnp.concatenate(k1_rows, axis=0))
    msgs[me] = jnp.concatenate(
        [
            jnp.where(live > 0.0, second_f, -1.0),
            jnp.concatenate(p_rows, axis=0),
            jnp.concatenate(q_rows, axis=0),
            tail,
        ],
        axis=0,
    ).astype(BF16)

    def out_copy(t, source):
        return pltpu.make_async_remote_copy(
            src_ref=msgs.at[source],
            dst_ref=msgs.at[source],
            send_sem=send_sem.at[t],
            recv_sem=recv_sem.at[source],
            device_id={"line": t},
            device_id_type=MESH,
        )

    def back_copy(t, source):
        return pltpu.make_async_remote_copy(
            src_ref=squares.at[t],
            dst_ref=landed.at[source],
            send_sem=back_send_sem.at[t],
            recv_sem=back_recv_sem.at[source],
            device_id={"line": t},
            device_id_type=MESH,
        )

    grad_scale = 2.0 / cands

    def tile(t, own):
        block = msgs[t].astype(F32)
        k2s = block[0:firsts]
        p = block[firsts : 2 * firsts]
        q = block[2 * firsts : 3 * firsts]
        tail = block[3 * firsts : 4 * firsts]
        k1s = jnp.broadcast_to(tail[:, width - 1 : width], (firsts, width))
        pair = tail[0:2] + tail[2:4]
        flow_row = jnp.where(
            lane_of < width // 2,
            jnp.broadcast_to(pair[0:1], (firsts, width)),
            pltpu.roll(jnp.broadcast_to(pair[1:2], (firsts, width)), width // 2, 1),
        )
        b1 = jnp.take_along_axis(flow_row, k1s.astype(jnp.int32), axis=1)
        b2 = jnp.take_along_axis(flow_row, jnp.maximum(k2s, 0.0).astype(jnp.int32), axis=1)
        alive = k2s >= 0.0
        det = 1.0 - p * q
        a1s = jnp.where(alive, (b1 + p * b2) / det, 0.0)
        a2s = jnp.where(alive, (b2 + q * b1) / det, 0.0)
        columns = lodf_ref[:, pl.ds(pl.multiple_of(t * width, width), width)]
        columns = jnp.concatenate([columns, columns], axis=1)
        a1_hi, a1_lo = split_bf16(a1s)
        a2_hi, a2_lo = split_bf16(a2s)
        k2_b, k1_b = k2s.astype(BF16), k1s.astype(BF16)
        zero_b = jnp.zeros((width, cands), BF16)
        one_b = jnp.ones((width, cands), BF16)
        spread = jnp.zeros((width, width), F32)
        first_sums = jnp.zeros((width, width), F32)
        pressure = jnp.zeros((width, cands), F32)
        square_rows = []
        for j0 in range(0, firsts, 2):
            hots, mixes = [], []
            for j in (j0, j0 + 1):
                row = slice(j, j + 1)
                at_two = line_b == jnp.broadcast_to(k2_b[row], (width, cands))
                at_one = line_b == jnp.broadcast_to(k1_b[row], (width, cands))

                def place(two, one):
                    two = jnp.broadcast_to(two, (width, cands))
                    one = jnp.broadcast_to(one, (width, cands))
                    return jnp.where(at_two, two, jnp.where(at_one, one, zero_b))

                hots.append(jnp.where(at_two, one_b, zero_b))
                mixes.append(
                    jnp.concatenate(
                        [place(a2_hi[row], a1_hi[row]), place(a2_lo[row], a1_lo[row])], axis=0
                    )
                )
            mixed = jnp.dot(
                columns, jnp.concatenate(mixes, axis=1), preferred_element_type=F32
            )
            weighted = []
            for i, j in enumerate((j0, j0 + 1)):
                row = slice(j, j + 1)
                x = mixed[:, i * cands : (i + 1) * cands]
                e = x - jnp.minimum(jnp.maximum(x, lower_ref[...]), upper_ref[...])
                if own:
                    keep = (line_f != k2s[row]) & (line_f != k1s[row]) & (k2s[row] >= 0.0)
                    e = jnp.where(keep, e, 0.0)
                square_rows.append(jnp.sum(e * e, axis=0, keepdims=True))
                pressure = pressure + e
                weighted.append((e * a2s[row]).astype(BF16))
                one_sum = jnp.sum(e * a1s[row], axis=1, keepdims=True)
                first_sums = jnp.where(lane_f == float(j), one_sum, first_sums)
            spread = spread + lax.dot_general(
                jnp.concatenate(weighted, axis=1),
                jnp.concatenate(hots, axis=1),
                (((1,), (1,)), ((), ())),
                preferred_element_type=F32,
            )
        hot_one = jnp.where(lane_of.astype(F32) == k1s, 1.0, 0.0)
        hot_one = jnp.concatenate([hot_one, jnp.zeros((width - firsts, width), F32)], axis=0)
        hot_one = hot_one.astype(BF16)
        sums_hi, sums_lo = split_bf16(first_sums)
        spread = spread + jnp.dot(
            jnp.concatenate([sums_hi, sums_lo], axis=1),
            jnp.concatenate([hot_one, hot_one], axis=0),
            preferred_element_type=F32,
        )
        grad_ref[:, pl.ds(pl.multiple_of(t * width, width), width)] = (
            spread * grad_scale
        ).astype(grad_ref.dtype)
        squares[t] = jnp.concatenate(square_rows, axis=0)
        if own:
            pres_acc[...] = pressure
            dead_ref[...] = jnp.zeros_like(dead_ref)
        else:
            pres_acc[...] += pressure
            dead_ref[...] += jnp.where(k2s < 0.0, 1.0, 0.0)

    loads[-1].wait()
    starts_late = chip >= half - 2

    @pl.when(jnp.logical_not(starts_late))
    def _():
        tile(me, True)

    pl.semaphore_wait(barrier, n - 1)
    for s in range(half - 1, 0, -1):
        there, _ = partners(half, chip, s)
        out_copy(2 * there + core, me).start()
        out_copy(2 * there + 1 - core, me).start()
    out_copy(mate, me).start()

    @pl.when(starts_late)
    def _():
        tile(me, True)

    out_copy(mate, mate).wait_recv()
    tile(mate, False)
    back_copy(mate, me).start()

    def screen(steps):
        tiles = []
        for s in steps:
            _, there = partners(half, chip, s)
            tiles += [2 * there + core, 2 * there + 1 - core]
        for t in tiles:
            out_copy(t, t).wait_recv()
        for t in tiles:
            tile(t, False)
        for t in tiles:
            back_copy(t, me).start()

    near = min(3, half - 1)
    order = list(range(1, near + 1)) + list(range(half - 1, near, -1))
    if half <= 8:
        early = min(3, half - 2)
        for i, s in enumerate(order):
            if i == early:
                s = jnp.where(chip == 0, s, chip)
            else:
                s = jnp.where(chip == s, order[early], s)
            screen([s])
    else:

        @pl.loop(0, half - 1)
        def _(i):
            screen([jnp.where(i < near, i + 1, half - 1 + near - i)])

    n_dead = jnp.sum(dead_ref[...])
    resting = -jnp.minimum(jnp.maximum(0.0, lower_ref[...]), upper_ref[...])
    lines_sum = jnp.sum(jnp.transpose(pres_acc[...]), axis=0, keepdims=True)
    rest_row = jnp.transpose(resting)[0:1, :]
    pairs = n * firsts * cands
    pres_ref[...] = (lines_sum - n_dead * rest_row) * (2.0 / pairs)

    landed[me] = squares[me]

    @pl.loop(1, n)
    def _(s):
        t = lax.rem(me + s, n)
        back_copy(t, t).wait_recv()

    total = jnp.sum(landed[...], axis=0)
    alive_now = msgs[me].astype(F32)[0:firsts] >= 0.0
    pen_ref[...] = jnp.where(alive_now, total, 0.0) / (n * width)

    @pl.loop(1, n)
    def _(s):
        t = lax.rem(me + s, n)
        out_copy(t, me).wait_send()
        back_copy(t, me).wait_send()


def hand_out(pen_in, pres_in, grad_in, pen_ref, pres_ref, grad_ref, sems):
    copies = [
        pltpu.make_async_copy(grad_in, grad_ref, sems.at[0]),
        pltpu.make_async_copy(pen_in, pen_ref, sems.at[1]),
        pltpu.make_async_copy(pres_in, pres_ref, sems.at[2]),
    ]
    for copy in copies:
        copy.start()
    for copy in copies:
        copy.wait()


def per_device(n, lodf, limits, base_flow, first_ids, second_ids, counts):
    width, lines = lodf.shape
    firsts, cands = second_ids.shape
    vmem = pl.BlockSpec(memory_space=pltpu.VMEM)
    anywhere = pl.BlockSpec(memory_space=pl.ANY)
    penalty, pressure, grad = pl.pallas_call(
        functools.partial(kernel, n),
        out_shape=(
            pltpu.VMEM((firsts, cands), F32),
            pltpu.VMEM((1, width), F32),
            pltpu.VMEM((width, lines), BF16),
        ),
        in_specs=[anywhere] * 6,
        out_specs=(vmem, vmem, vmem),
        scratch_shapes=[
            pltpu.VMEM((n, 4 * firsts, cands), BF16),
            pltpu.VMEM((n, firsts, cands), F32),
            pltpu.VMEM((n, firsts, cands), F32),
            pltpu.VMEM((width, cands), F32),
            pltpu.VMEM((width, cands), F32),
            pltpu.VMEM((width, cands), F32),
            pltpu.VMEM((firsts, cands), F32),
            pltpu.VMEM((width, lines), BF16),
            pltpu.VMEM((width, width), BF16),
            pltpu.VMEM((1, width), jnp.int32),
            pltpu.VMEM((1, width), F32),
            pltpu.VMEM((firsts, cands), jnp.int32),
            pltpu.SMEM((firsts,), jnp.int32),
            pltpu.SMEM((firsts,), jnp.int32),
            pltpu.SemaphoreType.DMA((n,)),
            pltpu.SemaphoreType.DMA((n,)),
            pltpu.SemaphoreType.DMA((n,)),
            pltpu.SemaphoreType.DMA((n,)),
            pltpu.SemaphoreType.DMA((7,)),
        ],
        compiler_params=pltpu.CompilerParams(collective_id=0, has_side_effects=True),
        name="screen",
    )(first_ids, counts, lodf, limits.reshape(1, width), base_flow.reshape(1, width), second_ids)
    penalty, pressure, grad = pl.pallas_call(
        hand_out,
        out_shape=(
            jax.ShapeDtypeStruct((firsts, cands), F32),
            jax.ShapeDtypeStruct((1, width), F32),
            jax.ShapeDtypeStruct((width, lines), BF16),
        ),
        in_specs=[anywhere] * 3,
        out_specs=(anywhere,) * 3,
        scratch_shapes=[pltpu.SemaphoreType.DMA((3,))],
        compiler_params=pltpu.CompilerParams(vmem_limit_bytes=1 << 20),
        name="hand_out",
    )(penalty, pressure, grad)
    return penalty, pressure.reshape(width), grad


def solution(mesh):
    return jax.shard_map(
        functools.partial(per_device, mesh.shape["line"]),
        mesh=mesh,
        in_specs=(
            P("line", None),
            P("line"),
            P(("groups", "line")),
            P(("groups", "line")),
            P(("groups", "line"), None),
            P(("groups", "line")),
        ),
        out_specs=(P(("groups", "line"), None), P(("groups", "line")), P(("groups", "line"), None)),
        check_vma=False,
    )
```

```python
import functools

import jax
import jax.numpy as jnp
from jax import lax
from jax.experimental import pallas as pl
from jax.experimental.pallas import tpu as pltpu
from jax.sharding import PartitionSpec as P


F32 = jnp.float32
BF16 = jnp.bfloat16
MESH = pl.DeviceIdType.MESH


def split_bf16(x):
    hi = x.astype(BF16)
    return hi, (x - hi.astype(F32)).astype(BF16)


def partners(half, chip, s):
    if half & (half - 1):
        return lax.rem(chip + half - s, half), lax.rem(chip + s, half)
    other, bit = 0, 1
    while bit < half:
        other = other + bit * lax.rem(chip // bit + s // bit, 2)
        bit *= 2
    return other, other


def kernel(
    n,
    first_hbm,
    counts_hbm,
    lodf_hbm,
    limits_hbm,
    base_hbm,
    second_hbm,
    pen_ref,
    pres_ref,
    grad_ref,
    msgs,
    squares,
    landed,
    pres_acc,
    lower_ref,
    upper_ref,
    dead_ref,
    lodf_ref,
    square_ref,
    limits_ref,
    base_ref,
    second_ref,
    first_ref,
    counts_ref,
    send_sem,
    recv_sem,
    back_send_sem,
    back_recv_sem,
    load_sem,
):
    me = lax.axis_index("line")
    width = lodf_ref.shape[0]
    firsts, cands = second_ref.shape
    anchor = pl.multiple_of(me * width, width)
    half = n // 2
    chip, core = me // 2, lax.rem(me, 2)
    mate = 2 * chip + 1 - core

    barrier = pltpu.get_barrier_semaphore()

    def greet(t):
        pl.semaphore_signal(barrier, inc=1, device_id={"line": t}, device_id_type=MESH)

    for s in range(half - 1, 0, -1):
        there, _ = partners(half, chip, s)
        greet(2 * there + core)
        greet(2 * there + 1 - core)
    greet(mate)

    loads = [
        pltpu.make_async_copy(lodf_hbm.at[:, pl.ds(anchor, width)], square_ref, load_sem.at[0]),
        pltpu.make_async_copy(first_hbm, first_ref, load_sem.at[1]),
        pltpu.make_async_copy(counts_hbm, counts_ref, load_sem.at[2]),
        pltpu.make_async_copy(second_hbm, second_ref, load_sem.at[3]),
        pltpu.make_async_copy(base_hbm, base_ref, load_sem.at[4]),
        pltpu.make_async_copy(limits_hbm, limits_ref, load_sem.at[5]),
        pltpu.make_async_copy(lodf_hbm, lodf_ref, load_sem.at[6]),
    ]
    for load in loads:
        load.start()

    line_f = lax.broadcasted_iota(jnp.int32, (width, cands), 0).astype(F32)
    lane_f = lax.broadcasted_iota(jnp.int32, (width, width), 1).astype(F32)
    line_b = line_f.astype(BF16)
    slot_row = lax.broadcasted_iota(jnp.int32, (1, cands), 1)
    row_of = lax.broadcasted_iota(jnp.int32, (firsts, width), 0)
    lane_of = lax.broadcasted_iota(jnp.int32, (firsts, width), 1)
    for load in loads[:-1]:
        load.wait()

    base_t = jnp.transpose(jnp.broadcast_to(base_ref[...], (cands, width)))
    limit_t = 0.01 * jnp.transpose(jnp.broadcast_to(limits_ref[...].astype(F32), (cands, width)))
    lower_ref[...] = -limit_t - base_t
    upper_ref[...] = limit_t - base_t
    square = square_ref[...]
    second_f = (second_ref[...] - anchor).astype(F32)
    k1_rows, p_rows, q_rows, live_rows = [], [], [], []
    for j in range(firsts):
        k1 = jnp.full((1, cands), first_ref[j] - anchor, jnp.int32).astype(F32)
        k2 = second_f[j : j + 1, :]
        mask_one = line_f == k1
        mask_two = line_f == k2
        by_two = jnp.dot(square, mask_two.astype(F32).astype(BF16), preferred_element_type=F32)
        by_one = jnp.dot(square, mask_one.astype(F32).astype(BF16), preferred_element_type=F32)
        p_rows.append(jnp.sum(jnp.where(mask_one, by_two, 0.0), axis=0, keepdims=True))
        q_rows.append(jnp.sum(jnp.where(mask_two, by_one, 0.0), axis=0, keepdims=True))
        k1_rows.append(k1)
        live_rows.append((slot_row < counts_ref[j]).astype(F32))
    live = jnp.concatenate(live_rows, axis=0)
    base_rows = jnp.broadcast_to(base_ref[...], (firsts, width))
    turned = pltpu.roll(base_rows, width // 2, 1)
    halves = jnp.where(lax.rem(row_of, 2) == 0, base_rows, turned)
    halves_hi = halves.astype(BF16).astype(F32)
    base_parts = jnp.where(row_of < 2, halves_hi, halves - halves_hi)
    tail = jnp.where(lane_of < width // 2, base_parts, jnp.concatenate(k1_rows, axis=0))
    msgs[me] = jnp.concatenate(
        [
            jnp.where(live > 0.0, second_f, -1.0),
            jnp.concatenate(p_rows, axis=0),
            jnp.concatenate(q_rows, axis=0),
            tail,
        ],
        axis=0,
    ).astype(BF16)

    def out_copy(t, source):
        return pltpu.make_async_remote_copy(
            src_ref=msgs.at[source],
            dst_ref=msgs.at[source],
            send_sem=send_sem.at[t],
            recv_sem=recv_sem.at[source],
            device_id={"line": t},
            device_id_type=MESH,
        )

    def back_copy(t, source):
        return pltpu.make_async_remote_copy(
            src_ref=squares.at[t],
            dst_ref=landed.at[source],
            send_sem=back_send_sem.at[t],
            recv_sem=back_recv_sem.at[source],
            device_id={"line": t},
            device_id_type=MESH,
        )

    grad_scale = 2.0 / cands

    def tile(t, own):
        block = msgs[t].astype(F32)
        k2s = block[0:firsts]
        p = block[firsts : 2 * firsts]
        q = block[2 * firsts : 3 * firsts]
        tail = block[3 * firsts : 4 * firsts]
        k1s = jnp.broadcast_to(tail[:, width - 1 : width], (firsts, width))
        pair = tail[0:2] + tail[2:4]
        flow_row = jnp.where(
            lane_of < width // 2,
            jnp.broadcast_to(pair[0:1], (firsts, width)),
            pltpu.roll(jnp.broadcast_to(pair[1:2], (firsts, width)), width // 2, 1),
        )
        b1 = jnp.take_along_axis(flow_row, k1s.astype(jnp.int32), axis=1)
        b2 = jnp.take_along_axis(flow_row, jnp.maximum(k2s, 0.0).astype(jnp.int32), axis=1)
        alive = k2s >= 0.0
        det = 1.0 - p * q
        a1s = jnp.where(alive, (b1 + p * b2) / det, 0.0)
        a2s = jnp.where(alive, (b2 + q * b1) / det, 0.0)
        columns = lodf_ref[:, pl.ds(pl.multiple_of(t * width, width), width)]
        columns = jnp.concatenate([columns, columns], axis=1)
        a1_hi, a1_lo = split_bf16(a1s)
        a2_hi, a2_lo = split_bf16(a2s)
        k2_b, k1_b = k2s.astype(BF16), k1s.astype(BF16)
        zero_b = jnp.zeros((width, cands), BF16)
        one_b = jnp.ones((width, cands), BF16)
        spread = jnp.zeros((width, width), F32)
        first_sums = jnp.zeros((width, width), F32)
        pressure = jnp.zeros((width, cands), F32)
        square_rows = []
        for j0 in range(0, firsts, 2):
            hots, mixes = [], []
            for j in (j0, j0 + 1):
                row = slice(j, j + 1)
                at_two = line_b == jnp.broadcast_to(k2_b[row], (width, cands))
                at_one = line_b == jnp.broadcast_to(k1_b[row], (width, cands))

                def place(two, one):
                    two = jnp.broadcast_to(two, (width, cands))
                    one = jnp.broadcast_to(one, (width, cands))
                    return jnp.where(at_two, two, jnp.where(at_one, one, zero_b))

                hots.append(jnp.where(at_two, one_b, zero_b))
                mixes.append(
                    jnp.concatenate(
                        [place(a2_hi[row], a1_hi[row]), place(a2_lo[row], a1_lo[row])], axis=0
                    )
                )
            mixed = jnp.dot(
                columns, jnp.concatenate(mixes, axis=1), preferred_element_type=F32
            )
            weighted = []
            for i, j in enumerate((j0, j0 + 1)):
                row = slice(j, j + 1)
                x = mixed[:, i * cands : (i + 1) * cands]
                e = x - jnp.minimum(jnp.maximum(x, lower_ref[...]), upper_ref[...])
                if own:
                    keep = (line_f != k2s[row]) & (line_f != k1s[row]) & (k2s[row] >= 0.0)
                    e = jnp.where(keep, e, 0.0)
                square_rows.append(jnp.sum(e * e, axis=0, keepdims=True))
                pressure = pressure + e
                weighted.append((e * a2s[row]).astype(BF16))
                one_sum = jnp.sum(e * a1s[row], axis=1, keepdims=True)
                first_sums = jnp.where(lane_f == float(j), one_sum, first_sums)
            spread = spread + lax.dot_general(
                jnp.concatenate(weighted, axis=1),
                jnp.concatenate(hots, axis=1),
                (((1,), (1,)), ((), ())),
                preferred_element_type=F32,
            )
        hot_one = jnp.where(lane_of.astype(F32) == k1s, 1.0, 0.0)
        hot_one = jnp.concatenate([hot_one, jnp.zeros((width - firsts, width), F32)], axis=0)
        hot_one = hot_one.astype(BF16)
        sums_hi, sums_lo = split_bf16(first_sums)
        spread = spread + jnp.dot(
            jnp.concatenate([sums_hi, sums_lo], axis=1),
            jnp.concatenate([hot_one, hot_one], axis=0),
            preferred_element_type=F32,
        )
        grad_ref[:, pl.ds(pl.multiple_of(t * width, width), width)] = (
            spread * grad_scale
        ).astype(grad_ref.dtype)
        squares[t] = jnp.concatenate(square_rows, axis=0)
        if own:
            pres_acc[...] = pressure
            dead_ref[...] = jnp.zeros_like(dead_ref)
        else:
            pres_acc[...] += pressure
            dead_ref[...] += jnp.where(k2s < 0.0, 1.0, 0.0)

    loads[-1].wait()
    starts_late = chip >= half - 2

    @pl.when(jnp.logical_not(starts_late))
    def _():
        tile(me, True)

    pl.semaphore_wait(barrier, n - 1)
    out_copy(mate, me).start()
    for s in range(half - 1, 0, -1):
        there, _ = partners(half, chip, s)
        out_copy(2 * there + core, me).start()
        out_copy(2 * there + 1 - core, me).start()

    @pl.when(starts_late)
    def _():
        tile(me, True)

    out_copy(mate, mate).wait_recv()
    tile(mate, False)
    back_copy(mate, me).start()

    def screen(steps):
        tiles = []
        for s in steps:
            _, there = partners(half, chip, s)
            tiles += [2 * there + core, 2 * there + 1 - core]
        for t in tiles:
            out_copy(t, t).wait_recv()
        for t in tiles:
            tile(t, False)
        for t in tiles:
            back_copy(t, me).start()

    near = min(3, half - 1)
    order = [1, 2, 3, 7, 5, 4, 6] if half == 8 else list(range(1, half))
    if half <= 8:
        early = min(3, half - 2)
        steps = []
        for i, s in enumerate(order):
            if i == early:
                steps.append(jnp.where(chip == 0, s, chip))
            else:
                steps.append(jnp.where(chip == s, order[early], s))
        second = chip + 1 - 2 * lax.rem(chip, 2)
        for i in range(early + 2, len(steps)):
            moved = steps[i] == second
            steps[early + 1], steps[i] = (
                jnp.where(moved, steps[i], steps[early + 1]),
                jnp.where(moved, steps[early + 1], steps[i]),
            )
        for first, last in ((0, 1), (1, 3), (3, 5), (5, 7)):
            screen(steps[first:last])
    else:

        @pl.loop(0, half - 1)
        def _(i):
            screen([jnp.where(i < near, i + 1, half - 1 + near - i)])

    n_dead = jnp.sum(dead_ref[...])
    resting = -jnp.minimum(jnp.maximum(0.0, lower_ref[...]), upper_ref[...])
    lines_sum = jnp.sum(jnp.transpose(pres_acc[...]), axis=0, keepdims=True)
    rest_row = jnp.transpose(resting)[0:1, :]
    pairs = n * firsts * cands
    pres_ref[...] = (lines_sum - n_dead * rest_row) * (2.0 / pairs)

    landed[me] = squares[me]

    @pl.loop(1, n)
    def _(s):
        t = lax.rem(me + s, n)
        back_copy(t, t).wait_recv()

    total = jnp.sum(landed[...], axis=0)
    alive_now = msgs[me].astype(F32)[0:firsts] >= 0.0
    pen_ref[...] = jnp.where(alive_now, total, 0.0) / (n * width)

    @pl.loop(1, n)
    def _(s):
        t = lax.rem(me + s, n)
        out_copy(t, me).wait_send()
        back_copy(t, me).wait_send()


def hand_out(pen_in, pres_in, grad_in, pen_ref, pres_ref, grad_ref, sems):
    copies = [
        pltpu.make_async_copy(grad_in, grad_ref, sems.at[0]),
        pltpu.make_async_copy(pen_in, pen_ref, sems.at[1]),
        pltpu.make_async_copy(pres_in, pres_ref, sems.at[2]),
    ]
    for copy in copies:
        copy.start()
    for copy in copies:
        copy.wait()


def per_device(n, lodf, limits, base_flow, first_ids, second_ids, counts):
    width, lines = lodf.shape
    firsts, cands = second_ids.shape
    vmem = pl.BlockSpec(memory_space=pltpu.VMEM)
    anywhere = pl.BlockSpec(memory_space=pl.ANY)
    penalty, pressure, grad = pl.pallas_call(
        functools.partial(kernel, n),
        out_shape=(
            pltpu.VMEM((firsts, cands), F32),
            pltpu.VMEM((1, width), F32),
            pltpu.VMEM((width, lines), BF16),
        ),
        in_specs=[anywhere] * 6,
        out_specs=(vmem, vmem, vmem),
        scratch_shapes=[
            pltpu.VMEM((n, 4 * firsts, cands), BF16),
            pltpu.VMEM((n, firsts, cands), F32),
            pltpu.VMEM((n, firsts, cands), F32),
            pltpu.VMEM((width, cands), F32),
            pltpu.VMEM((width, cands), F32),
            pltpu.VMEM((width, cands), F32),
            pltpu.VMEM((firsts, cands), F32),
            pltpu.VMEM((width, lines), BF16),
            pltpu.VMEM((width, width), BF16),
            pltpu.VMEM((1, width), jnp.int32),
            pltpu.VMEM((1, width), F32),
            pltpu.VMEM((firsts, cands), jnp.int32),
            pltpu.SMEM((firsts,), jnp.int32),
            pltpu.SMEM((firsts,), jnp.int32),
            pltpu.SemaphoreType.DMA((n,)),
            pltpu.SemaphoreType.DMA((n,)),
            pltpu.SemaphoreType.DMA((n,)),
            pltpu.SemaphoreType.DMA((n,)),
            pltpu.SemaphoreType.DMA((7,)),
        ],
        compiler_params=pltpu.CompilerParams(collective_id=0, has_side_effects=True),
        name="screen",
    )(first_ids, counts, lodf, limits.reshape(1, width), base_flow.reshape(1, width), second_ids)
    penalty, pressure, grad = pl.pallas_call(
        hand_out,
        out_shape=(
            jax.ShapeDtypeStruct((firsts, cands), F32),
            jax.ShapeDtypeStruct((1, width), F32),
            jax.ShapeDtypeStruct((width, lines), BF16),
        ),
        in_specs=[anywhere] * 3,
        out_specs=(anywhere,) * 3,
        scratch_shapes=[pltpu.SemaphoreType.DMA((3,))],
        compiler_params=pltpu.CompilerParams(vmem_limit_bytes=1 << 20),
        name="hand_out",
    )(penalty, pressure, grad)
    return penalty, pressure.reshape(width), grad


def solution(mesh):
    return jax.shard_map(
        functools.partial(per_device, mesh.shape["line"]),
        mesh=mesh,
        in_specs=(
            P("line", None),
            P("line"),
            P(("groups", "line")),
            P(("groups", "line")),
            P(("groups", "line"), None),
            P(("groups", "line")),
        ),
        out_specs=(P(("groups", "line"), None), P(("groups", "line")), P(("groups", "line"), None)),
        check_vma=False,
    )
```

```python
import functools

import jax
import jax.numpy as jnp
from jax import lax
from jax.experimental import pallas as pl
from jax.experimental.pallas import tpu as pltpu
from jax.sharding import PartitionSpec as P


F32 = jnp.float32
BF16 = jnp.bfloat16
MESH = pl.DeviceIdType.MESH


def split_bf16(x):
    hi = x.astype(BF16)
    return hi, (x - hi.astype(F32)).astype(BF16)


def partners(half, chip, s):
    if half & (half - 1):
        return lax.rem(chip + half - s, half), lax.rem(chip + s, half)
    other, bit = 0, 1
    while bit < half:
        other = other + bit * lax.rem(chip // bit + s // bit, 2)
        bit *= 2
    return other, other


def kernel(
    n,
    first_hbm,
    counts_hbm,
    lodf_hbm,
    limits_hbm,
    base_hbm,
    second_hbm,
    pen_ref,
    pres_ref,
    grad_ref,
    msgs,
    squares,
    landed,
    pres_acc,
    lower_ref,
    upper_ref,
    dead_ref,
    lodf_ref,
    square_ref,
    limits_ref,
    base_ref,
    second_ref,
    first_ref,
    counts_ref,
    send_sem,
    recv_sem,
    back_send_sem,
    back_recv_sem,
    load_sem,
):
    me = lax.axis_index("line")
    width = lodf_ref.shape[0]
    firsts, cands = second_ref.shape
    anchor = pl.multiple_of(me * width, width)
    half = n // 2
    chip, core = me // 2, lax.rem(me, 2)
    mate = 2 * chip + 1 - core

    barrier = pltpu.get_barrier_semaphore()

    def greet(t):
        pl.semaphore_signal(barrier, inc=1, device_id={"line": t}, device_id_type=MESH)

    for s in range(half - 1, 0, -1):
        there, _ = partners(half, chip, s)
        greet(2 * there + core)
        greet(2 * there + 1 - core)
    greet(mate)

    loads = [
        pltpu.make_async_copy(lodf_hbm.at[:, pl.ds(anchor, width)], square_ref, load_sem.at[0]),
        pltpu.make_async_copy(first_hbm, first_ref, load_sem.at[1]),
        pltpu.make_async_copy(counts_hbm, counts_ref, load_sem.at[2]),
        pltpu.make_async_copy(second_hbm, second_ref, load_sem.at[3]),
        pltpu.make_async_copy(base_hbm, base_ref, load_sem.at[4]),
        pltpu.make_async_copy(limits_hbm, limits_ref, load_sem.at[5]),
        pltpu.make_async_copy(lodf_hbm, lodf_ref, load_sem.at[6]),
    ]
    for load in loads:
        load.start()

    line_f = lax.broadcasted_iota(jnp.int32, (width, cands), 0).astype(F32)
    lane_f = lax.broadcasted_iota(jnp.int32, (width, width), 1).astype(F32)
    line_b = line_f.astype(BF16)
    slot_row = lax.broadcasted_iota(jnp.int32, (1, cands), 1)
    row_of = lax.broadcasted_iota(jnp.int32, (firsts, width), 0)
    lane_of = lax.broadcasted_iota(jnp.int32, (firsts, width), 1)
    for load in loads[:-1]:
        load.wait()

    base_t = jnp.transpose(jnp.broadcast_to(base_ref[...], (cands, width)))
    limit_t = 0.01 * jnp.transpose(jnp.broadcast_to(limits_ref[...].astype(F32), (cands, width)))
    lower_ref[...] = -limit_t - base_t
    upper_ref[...] = limit_t - base_t
    square = square_ref[...]
    second_f = (second_ref[...] - anchor).astype(F32)
    k1_rows, p_rows, q_rows, live_rows = [], [], [], []
    for j in range(firsts):
        k1 = jnp.full((1, cands), first_ref[j] - anchor, jnp.int32).astype(F32)
        k2 = second_f[j : j + 1, :]
        mask_one = line_f == k1
        mask_two = line_f == k2
        by_two = jnp.dot(square, mask_two.astype(F32).astype(BF16), preferred_element_type=F32)
        by_one = jnp.dot(square, mask_one.astype(F32).astype(BF16), preferred_element_type=F32)
        p_rows.append(jnp.sum(jnp.where(mask_one, by_two, 0.0), axis=0, keepdims=True))
        q_rows.append(jnp.sum(jnp.where(mask_two, by_one, 0.0), axis=0, keepdims=True))
        k1_rows.append(k1)
        live_rows.append((slot_row < counts_ref[j]).astype(F32))
    live = jnp.concatenate(live_rows, axis=0)
    base_rows = jnp.broadcast_to(base_ref[...], (firsts, width))
    turned = pltpu.roll(base_rows, width // 2, 1)
    halves = jnp.where(lax.rem(row_of, 2) == 0, base_rows, turned)
    halves_hi = halves.astype(BF16).astype(F32)
    base_parts = jnp.where(row_of < 2, halves_hi, halves - halves_hi)
    tail = jnp.where(lane_of < width // 2, base_parts, jnp.concatenate(k1_rows, axis=0))
    msgs[me] = jnp.concatenate(
        [
            jnp.where(live > 0.0, second_f, -1.0),
            jnp.concatenate(p_rows, axis=0),
            jnp.concatenate(q_rows, axis=0),
            tail,
        ],
        axis=0,
    ).astype(BF16)

    def out_copy(t, source):
        return pltpu.make_async_remote_copy(
            src_ref=msgs.at[source],
            dst_ref=msgs.at[source],
            send_sem=send_sem.at[t],
            recv_sem=recv_sem.at[source],
            device_id={"line": t},
            device_id_type=MESH,
        )

    def back_copy(t, source):
        return pltpu.make_async_remote_copy(
            src_ref=squares.at[t],
            dst_ref=landed.at[source],
            send_sem=back_send_sem.at[t],
            recv_sem=back_recv_sem.at[source],
            device_id={"line": t},
            device_id_type=MESH,
        )

    grad_scale = 2.0 / cands

    def tile(t, own):
        block = msgs[t].astype(F32)
        k2s = block[0:firsts]
        p = block[firsts : 2 * firsts]
        q = block[2 * firsts : 3 * firsts]
        tail = block[3 * firsts : 4 * firsts]
        k1s = jnp.broadcast_to(tail[:, width - 1 : width], (firsts, width))
        pair = tail[0:2] + tail[2:4]
        flow_row = jnp.where(
            lane_of < width // 2,
            jnp.broadcast_to(pair[0:1], (firsts, width)),
            pltpu.roll(jnp.broadcast_to(pair[1:2], (firsts, width)), width // 2, 1),
        )
        b1 = jnp.take_along_axis(flow_row, k1s.astype(jnp.int32), axis=1)
        b2 = jnp.take_along_axis(flow_row, jnp.maximum(k2s, 0.0).astype(jnp.int32), axis=1)
        alive = k2s >= 0.0
        det = 1.0 - p * q
        a1s = jnp.where(alive, (b1 + p * b2) / det, 0.0)
        a2s = jnp.where(alive, (b2 + q * b1) / det, 0.0)
        columns = lodf_ref[:, pl.ds(pl.multiple_of(t * width, width), width)]
        columns = jnp.concatenate([columns, columns], axis=1)
        a1_hi, a1_lo = split_bf16(a1s)
        a2_hi, a2_lo = split_bf16(a2s)
        k2_b, k1_b = k2s.astype(BF16), k1s.astype(BF16)
        zero_b = jnp.zeros((width, cands), BF16)
        one_b = jnp.ones((width, cands), BF16)
        spread = jnp.zeros((width, width), F32)
        first_sums = jnp.zeros((width, width), F32)
        pressure = jnp.zeros((width, cands), F32)
        square_rows = []
        for j0 in range(0, firsts, 2):
            hots, mixes = [], []
            for j in (j0, j0 + 1):
                row = slice(j, j + 1)
                at_two = line_b == jnp.broadcast_to(k2_b[row], (width, cands))
                at_one = line_b == jnp.broadcast_to(k1_b[row], (width, cands))

                hot = jnp.where(at_two, one_b, zero_b)

                def place(two, one):
                    two = jnp.broadcast_to(two, (width, cands))
                    one = jnp.broadcast_to(one, (width, cands))
                    return hot * two + jnp.where(at_one, one, zero_b)

                hots.append(hot)
                mixes.append(
                    jnp.concatenate(
                        [place(a2_hi[row], a1_hi[row]), place(a2_lo[row], a1_lo[row])], axis=0
                    )
                )
            mixed = jnp.dot(
                columns, jnp.concatenate(mixes, axis=1), preferred_element_type=F32
            )
            weighted = []
            for i, j in enumerate((j0, j0 + 1)):
                row = slice(j, j + 1)
                x = mixed[:, i * cands : (i + 1) * cands]
                e = x - jnp.minimum(jnp.maximum(x, lower_ref[...]), upper_ref[...])
                if own:
                    keep = (line_f != k2s[row]) & (line_f != k1s[row]) & (k2s[row] >= 0.0)
                    e = jnp.where(keep, e, 0.0)
                square_rows.append(jnp.sum(e * e, axis=0, keepdims=True))
                pressure = pressure + e
                weighted.append((e * a2s[row]).astype(BF16))
                one_sum = jnp.sum(e * a1s[row], axis=1, keepdims=True)
                first_sums = jnp.where(lane_f == float(j), one_sum, first_sums)
            spread = spread + lax.dot_general(
                jnp.concatenate(weighted, axis=1),
                jnp.concatenate(hots, axis=1),
                (((1,), (1,)), ((), ())),
                preferred_element_type=F32,
            )
        hot_one = jnp.where(lane_of.astype(F32) == k1s, 1.0, 0.0)
        hot_one = jnp.concatenate([hot_one, jnp.zeros((width - firsts, width), F32)], axis=0)
        hot_one = hot_one.astype(BF16)
        sums_hi, sums_lo = split_bf16(first_sums)
        spread = spread + jnp.dot(
            jnp.concatenate([sums_hi, sums_lo], axis=1),
            jnp.concatenate([hot_one, hot_one], axis=0),
            preferred_element_type=F32,
        )
        grad_ref[:, pl.ds(pl.multiple_of(t * width, width), width)] = (
            spread * grad_scale
        ).astype(grad_ref.dtype)
        squares[t] = jnp.concatenate(square_rows, axis=0)
        if own:
            pres_acc[...] = pressure
            dead_ref[...] = jnp.zeros_like(dead_ref)
        else:
            pres_acc[...] += pressure
            dead_ref[...] += jnp.where(k2s < 0.0, 1.0, 0.0)

    loads[-1].wait()
    starts_late = chip >= half - 2

    @pl.when(jnp.logical_not(starts_late))
    def _():
        tile(me, True)

    pl.semaphore_wait(barrier, n - 1)
    out_copy(mate, me).start()
    for s in range(half - 1, 0, -1):
        there, _ = partners(half, chip, s)
        out_copy(2 * there + core, me).start()
        out_copy(2 * there + 1 - core, me).start()

    @pl.when(starts_late)
    def _():
        tile(me, True)

    out_copy(mate, mate).wait_recv()
    tile(mate, False)
    back_copy(mate, me).start()

    def screen(steps):
        tiles = []
        for s in steps:
            _, there = partners(half, chip, s)
            tiles += [2 * there + core, 2 * there + 1 - core]
        for t in tiles:
            out_copy(t, t).wait_recv()
        for t in tiles:
            tile(t, False)
        for t in tiles:
            back_copy(t, me).start()

    near = min(3, half - 1)
    order = [1, 2, 3, 7, 5, 4, 6] if half == 8 else list(range(1, half))
    if half <= 8:
        early = min(3, half - 2)
        steps = []
        for i, s in enumerate(order):
            if i == early:
                steps.append(jnp.where(chip == 0, s, chip))
            else:
                steps.append(jnp.where(chip == s, order[early], s))
        second = chip + 1 - 2 * lax.rem(chip, 2)
        for i in range(early + 2, len(steps)):
            moved = steps[i] == second
            steps[early + 1], steps[i] = (
                jnp.where(moved, steps[i], steps[early + 1]),
                jnp.where(moved, steps[early + 1], steps[i]),
            )
        for first, last in ((0, 1), (1, 3), (3, 5), (5, 7)):
            screen(steps[first:last])
    else:

        @pl.loop(0, half - 1)
        def _(i):
            screen([jnp.where(i < near, i + 1, half - 1 + near - i)])

    n_dead = jnp.sum(dead_ref[...])
    resting = -jnp.minimum(jnp.maximum(0.0, lower_ref[...]), upper_ref[...])
    lines_sum = jnp.sum(jnp.transpose(pres_acc[...]), axis=0, keepdims=True)
    rest_row = jnp.transpose(resting)[0:1, :]
    pairs = n * firsts * cands
    pres_ref[...] = (lines_sum - n_dead * rest_row) * (2.0 / pairs)

    landed[me] = squares[me]
    alive_now = jnp.where(msgs[me].astype(F32)[0:firsts] >= 0.0, 1.0 / (n * width), 0.0)

    @pl.loop(1, n)
    def _(s):
        t = lax.rem(me + s, n)
        out_copy(t, me).wait_send()
        back_copy(t, me).wait_send()

    @pl.loop(1, n)
    def _(s):
        t = lax.rem(me + s, n)
        back_copy(t, t).wait_recv()

    pen_ref[...] = jnp.sum(landed[...], axis=0) * alive_now


def hand_out(pen_in, pres_in, grad_in, pen_ref, pres_ref, grad_ref, sems):
    copies = [
        pltpu.make_async_copy(grad_in, grad_ref, sems.at[0]),
        pltpu.make_async_copy(pen_in, pen_ref, sems.at[1]),
        pltpu.make_async_copy(pres_in, pres_ref, sems.at[2]),
    ]
    for copy in copies:
        copy.start()
    for copy in copies:
        copy.wait()


def per_device(n, lodf, limits, base_flow, first_ids, second_ids, counts):
    width, lines = lodf.shape
    firsts, cands = second_ids.shape
    vmem = pl.BlockSpec(memory_space=pltpu.VMEM)
    anywhere = pl.BlockSpec(memory_space=pl.ANY)
    penalty, pressure, grad = pl.pallas_call(
        functools.partial(kernel, n),
        out_shape=(
            pltpu.VMEM((firsts, cands), F32),
            pltpu.VMEM((1, width), F32),
            pltpu.VMEM((width, lines), BF16),
        ),
        in_specs=[anywhere] * 6,
        out_specs=(vmem, vmem, vmem),
        scratch_shapes=[
            pltpu.VMEM((n, 4 * firsts, cands), BF16),
            pltpu.VMEM((n, firsts, cands), F32),
            pltpu.VMEM((n, firsts, cands), F32),
            pltpu.VMEM((width, cands), F32),
            pltpu.VMEM((width, cands), F32),
            pltpu.VMEM((width, cands), F32),
            pltpu.VMEM((firsts, cands), F32),
            pltpu.VMEM((width, lines), BF16),
            pltpu.VMEM((width, width), BF16),
            pltpu.VMEM((1, width), jnp.int32),
            pltpu.VMEM((1, width), F32),
            pltpu.VMEM((firsts, cands), jnp.int32),
            pltpu.SMEM((firsts,), jnp.int32),
            pltpu.SMEM((firsts,), jnp.int32),
            pltpu.SemaphoreType.DMA((n,)),
            pltpu.SemaphoreType.DMA((n,)),
            pltpu.SemaphoreType.DMA((n,)),
            pltpu.SemaphoreType.DMA((n,)),
            pltpu.SemaphoreType.DMA((7,)),
        ],
        compiler_params=pltpu.CompilerParams(collective_id=0, has_side_effects=True),
        name="screen",
    )(first_ids, counts, lodf, limits.reshape(1, width), base_flow.reshape(1, width), second_ids)
    penalty, pressure, grad = pl.pallas_call(
        hand_out,
        out_shape=(
            jax.ShapeDtypeStruct((firsts, cands), F32),
            jax.ShapeDtypeStruct((1, width), F32),
            jax.ShapeDtypeStruct((width, lines), BF16),
        ),
        in_specs=[anywhere] * 3,
        out_specs=(anywhere,) * 3,
        scratch_shapes=[pltpu.SemaphoreType.DMA((3,))],
        compiler_params=pltpu.CompilerParams(vmem_limit_bytes=1 << 20),
        name="hand_out",
    )(penalty, pressure, grad)
    return penalty, pressure.reshape(width), grad


def solution(mesh):
    return jax.shard_map(
        functools.partial(per_device, mesh.shape["line"]),
        mesh=mesh,
        in_specs=(
            P("line", None),
            P("line"),
            P(("groups", "line")),
            P(("groups", "line")),
            P(("groups", "line"), None),
            P(("groups", "line")),
        ),
        out_specs=(P(("groups", "line"), None), P(("groups", "line")), P(("groups", "line"), None)),
        check_vma=False,
    )
```

```python
import functools

import jax
import jax.numpy as jnp
from jax import lax
from jax.experimental import pallas as pl
from jax.experimental.pallas import tpu as pltpu
from jax.sharding import PartitionSpec as P


F32 = jnp.float32
BF16 = jnp.bfloat16
MESH = pl.DeviceIdType.MESH


def split_bf16(x):
    hi = x.astype(BF16)
    return hi, (x - hi.astype(F32)).astype(BF16)


def partners(half, chip, s):
    if half & (half - 1):
        return lax.rem(chip + half - s, half), lax.rem(chip + s, half)
    other, bit = 0, 1
    while bit < half:
        other = other + bit * lax.rem(chip // bit + s // bit, 2)
        bit *= 2
    return other, other


def kernel(
    n,
    first_hbm,
    counts_hbm,
    lodf_hbm,
    limits_hbm,
    base_hbm,
    second_hbm,
    pen_ref,
    pres_ref,
    grad_ref,
    msgs,
    squares,
    landed,
    pres_acc,
    lower_ref,
    upper_ref,
    dead_ref,
    lodf_ref,
    square_ref,
    limits_ref,
    base_ref,
    second_ref,
    first_ref,
    counts_ref,
    send_sem,
    recv_sem,
    back_send_sem,
    back_recv_sem,
    load_sem,
):
    me = lax.axis_index("line")
    width = lodf_ref.shape[0]
    firsts, cands = second_ref.shape
    anchor = pl.multiple_of(me * width, width)
    half = n // 2
    chip, core = me // 2, lax.rem(me, 2)
    mate = 2 * chip + 1 - core

    barrier = pltpu.get_barrier_semaphore()

    def greet(t):
        pl.semaphore_signal(barrier, inc=1, device_id={"line": t}, device_id_type=MESH)

    for s in range(half - 1, 0, -1):
        there, _ = partners(half, chip, s)
        greet(2 * there + core)
        greet(2 * there + 1 - core)
    greet(mate)

    loads = [
        pltpu.make_async_copy(lodf_hbm.at[:, pl.ds(anchor, width)], square_ref, load_sem.at[0]),
        pltpu.make_async_copy(first_hbm, first_ref, load_sem.at[1]),
        pltpu.make_async_copy(counts_hbm, counts_ref, load_sem.at[2]),
        pltpu.make_async_copy(second_hbm, second_ref, load_sem.at[3]),
        pltpu.make_async_copy(base_hbm, base_ref, load_sem.at[4]),
        pltpu.make_async_copy(limits_hbm, limits_ref, load_sem.at[5]),
        pltpu.make_async_copy(lodf_hbm, lodf_ref, load_sem.at[6]),
    ]
    for load in loads:
        load.start()

    line_f = lax.broadcasted_iota(jnp.int32, (width, cands), 0).astype(F32)
    lane_f = lax.broadcasted_iota(jnp.int32, (width, width), 1).astype(F32)
    line_b = line_f.astype(BF16)
    slot_row = lax.broadcasted_iota(jnp.int32, (1, cands), 1)
    row_of = lax.broadcasted_iota(jnp.int32, (firsts, width), 0)
    lane_of = lax.broadcasted_iota(jnp.int32, (firsts, width), 1)
    for load in loads[:-1]:
        load.wait()

    base_t = jnp.transpose(jnp.broadcast_to(base_ref[...], (cands, width)))
    limit_t = 0.01 * jnp.transpose(jnp.broadcast_to(limits_ref[...].astype(F32), (cands, width)))
    lower_ref[...] = -limit_t - base_t
    upper_ref[...] = limit_t - base_t
    square = square_ref[...]
    second_f = (second_ref[...] - anchor).astype(F32)
    k1_rows, p_rows, q_rows, live_rows = [], [], [], []
    for j in range(firsts):
        k1 = jnp.full((1, cands), first_ref[j] - anchor, jnp.int32).astype(F32)
        k2 = second_f[j : j + 1, :]
        mask_one = line_f == k1
        mask_two = line_f == k2
        by_two = jnp.dot(square, mask_two.astype(F32).astype(BF16), preferred_element_type=F32)
        by_one = jnp.dot(square, mask_one.astype(F32).astype(BF16), preferred_element_type=F32)
        p_rows.append(jnp.sum(jnp.where(mask_one, by_two, 0.0), axis=0, keepdims=True))
        q_rows.append(jnp.sum(jnp.where(mask_two, by_one, 0.0), axis=0, keepdims=True))
        k1_rows.append(k1)
        live_rows.append((slot_row < counts_ref[j]).astype(F32))
    live = jnp.concatenate(live_rows, axis=0)
    base_rows = jnp.broadcast_to(base_ref[...], (firsts, width))
    turned = pltpu.roll(base_rows, width // 2, 1)
    halves = jnp.where(lax.rem(row_of, 2) == 0, base_rows, turned)
    halves_hi = halves.astype(BF16).astype(F32)
    base_parts = jnp.where(row_of < 2, halves_hi, halves - halves_hi)
    tail = jnp.where(lane_of < width // 2, base_parts, jnp.concatenate(k1_rows, axis=0))
    msgs[me] = jnp.concatenate(
        [
            jnp.where(live > 0.0, second_f, -1.0),
            jnp.concatenate(p_rows, axis=0),
            jnp.concatenate(q_rows, axis=0),
            tail,
        ],
        axis=0,
    ).astype(BF16)

    def out_copy(t, source):
        return pltpu.make_async_remote_copy(
            src_ref=msgs.at[source],
            dst_ref=msgs.at[source],
            send_sem=send_sem.at[t],
            recv_sem=recv_sem.at[source],
            device_id={"line": t},
            device_id_type=MESH,
        )

    def back_copy(t, source):
        return pltpu.make_async_remote_copy(
            src_ref=squares.at[t],
            dst_ref=landed.at[source],
            send_sem=back_send_sem.at[t],
            recv_sem=back_recv_sem.at[source],
            device_id={"line": t},
            device_id_type=MESH,
        )

    grad_scale = 2.0 / cands

    def add_piece(spread, weighted, hots):
        return spread + lax.dot_general(
            weighted, hots, (((1,), (1,)), ((), ())), preferred_element_type=F32
        )

    def tile(t, own, later=False):
        block = msgs[t].astype(F32)
        k2s = block[0:firsts]
        p = block[firsts : 2 * firsts]
        q = block[2 * firsts : 3 * firsts]
        tail = block[3 * firsts : 4 * firsts]
        k1s = jnp.broadcast_to(tail[:, width - 1 : width], (firsts, width))
        pair = tail[0:2] + tail[2:4]
        flow_row = jnp.where(
            lane_of < width // 2,
            jnp.broadcast_to(pair[0:1], (firsts, width)),
            pltpu.roll(jnp.broadcast_to(pair[1:2], (firsts, width)), width // 2, 1),
        )
        b1 = jnp.take_along_axis(flow_row, k1s.astype(jnp.int32), axis=1)
        b2 = jnp.take_along_axis(flow_row, jnp.maximum(k2s, 0.0).astype(jnp.int32), axis=1)
        alive = k2s >= 0.0
        det = 1.0 - p * q
        a1s = jnp.where(alive, (b1 + p * b2) / det, 0.0)
        a2s = jnp.where(alive, (b2 + q * b1) / det, 0.0)
        columns = lodf_ref[:, pl.ds(pl.multiple_of(t * width, width), width)]
        columns = jnp.concatenate([columns, columns], axis=1)
        a1_hi, a1_lo = split_bf16(a1s)
        a2_hi, a2_lo = split_bf16(a2s)
        k2_b, k1_b = k2s.astype(BF16), k1s.astype(BF16)
        zero_b = jnp.zeros((width, cands), BF16)
        one_b = jnp.ones((width, cands), BF16)
        spread = jnp.zeros((width, width), F32)
        first_sums = jnp.zeros((width, width), F32)
        pressure = jnp.zeros((width, cands), F32)
        square_rows, pieces = [], []
        for j0 in range(0, firsts, 2):
            hots, mixes = [], []
            for j in (j0, j0 + 1):
                row = slice(j, j + 1)
                at_two = line_b == jnp.broadcast_to(k2_b[row], (width, cands))
                at_one = line_b == jnp.broadcast_to(k1_b[row], (width, cands))

                hot = jnp.where(at_two, one_b, zero_b)

                def place(two, one):
                    two = jnp.broadcast_to(two, (width, cands))
                    one = jnp.broadcast_to(one, (width, cands))
                    return hot * two + jnp.where(at_one, one, zero_b)

                hots.append(hot)
                mixes.append(
                    jnp.concatenate(
                        [place(a2_hi[row], a1_hi[row]), place(a2_lo[row], a1_lo[row])], axis=0
                    )
                )
            mixed = jnp.dot(
                columns, jnp.concatenate(mixes, axis=1), preferred_element_type=F32
            )
            weighted = []
            for i, j in enumerate((j0, j0 + 1)):
                row = slice(j, j + 1)
                x = mixed[:, i * cands : (i + 1) * cands]
                e = x - jnp.minimum(jnp.maximum(x, lower_ref[...]), upper_ref[...])
                if own:
                    keep = (line_f != k2s[row]) & (line_f != k1s[row]) & (k2s[row] >= 0.0)
                    e = jnp.where(keep, e, 0.0)
                square_rows.append(jnp.sum(e * e, axis=0, keepdims=True))
                pressure = pressure + e
                weighted.append((e * a2s[row]).astype(BF16))
                one_sum = jnp.sum(e * a1s[row], axis=1, keepdims=True)
                first_sums = jnp.where(lane_f == float(j), one_sum, first_sums)
            pieces.append((jnp.concatenate(weighted, axis=1), jnp.concatenate(hots, axis=1)))
            if not later:
                spread = add_piece(spread, *pieces.pop())
        squares[t] = jnp.concatenate(square_rows, axis=0)

        def finish(spread):
            for piece in pieces:
                spread = add_piece(spread, *piece)
            hot_one = jnp.where(lane_of.astype(F32) == k1s, 1.0, 0.0)
            hot_one = jnp.concatenate([hot_one, jnp.zeros((width - firsts, width), F32)], axis=0)
            hot_one = hot_one.astype(BF16)
            sums_hi, sums_lo = split_bf16(first_sums)
            spread = spread + jnp.dot(
                jnp.concatenate([sums_hi, sums_lo], axis=1),
                jnp.concatenate([hot_one, hot_one], axis=0),
                preferred_element_type=F32,
            )
            grad_ref[:, pl.ds(pl.multiple_of(t * width, width), width)] = (
                spread * grad_scale
            ).astype(grad_ref.dtype)
            if own:
                pres_acc[...] = pressure
                dead_ref[...] = jnp.zeros_like(dead_ref)
            else:
                pres_acc[...] += pressure
                dead_ref[...] += jnp.where(k2s < 0.0, 1.0, 0.0)

        if later:
            return functools.partial(finish, spread)
        finish(spread)
        return None

    loads[-1].wait()
    starts_late = chip >= half - 2

    @pl.when(jnp.logical_not(starts_late))
    def _():
        tile(me, True)

    pl.semaphore_wait(barrier, n - 1)
    out_copy(mate, me).start()
    for s in range(half - 1, 0, -1):
        there, _ = partners(half, chip, s)
        out_copy(2 * there + core, me).start()
        out_copy(2 * there + 1 - core, me).start()

    @pl.when(starts_late)
    def _():
        tile(me, True)

    out_copy(mate, mate).wait_recv()
    tile(mate, False)
    back_copy(mate, me).start()

    def screen(steps, later=False):
        tiles = []
        for s in steps:
            _, there = partners(half, chip, s)
            tiles += [2 * there + core, 2 * there + 1 - core]
        for t in tiles:
            out_copy(t, t).wait_recv()
        finishes = [tile(t, False, later) for t in tiles]
        for t in tiles:
            back_copy(t, me).start()
        for finish in finishes:
            if later:
                finish()

    near = min(3, half - 1)
    order = [1, 2, 3, 7, 5, 4, 6] if half == 8 else list(range(1, half))
    if half <= 8:
        early = min(3, half - 2)
        steps = []
        for i, s in enumerate(order):
            if i == early:
                steps.append(jnp.where(chip == 0, s, chip))
            else:
                steps.append(jnp.where(chip == s, order[early], s))
        second = chip + 1 - 2 * lax.rem(chip, 2)
        for i in range(early + 2, len(steps)):
            moved = steps[i] == second
            steps[early + 1], steps[i] = (
                jnp.where(moved, steps[i], steps[early + 1]),
                jnp.where(moved, steps[early + 1], steps[i]),
            )
        for first, last in ((0, 1), (1, 3), (3, 5), (5, 7)):
            screen(steps[first:last], first >= early)
    else:

        @pl.loop(0, half - 1)
        def _(i):
            screen([jnp.where(i < near, i + 1, half - 1 + near - i)])

    n_dead = jnp.sum(dead_ref[...])
    resting = -jnp.minimum(jnp.maximum(0.0, lower_ref[...]), upper_ref[...])
    lines_sum = jnp.sum(jnp.transpose(pres_acc[...]), axis=0, keepdims=True)
    rest_row = jnp.transpose(resting)[0:1, :]
    pairs = n * firsts * cands
    pres_ref[...] = (lines_sum - n_dead * rest_row) * (2.0 / pairs)

    landed[me] = squares[me]
    alive_now = jnp.where(msgs[me].astype(F32)[0:firsts] >= 0.0, 1.0 / (n * width), 0.0)

    @pl.loop(1, n)
    def _(s):
        t = lax.rem(me + s, n)
        out_copy(t, me).wait_send()
        back_copy(t, me).wait_send()

    @pl.loop(1, n)
    def _(s):
        t = lax.rem(me + s, n)
        back_copy(t, t).wait_recv()

    pen_ref[...] = jnp.sum(landed[...], axis=0) * alive_now


def hand_out(pen_in, pres_in, grad_in, pen_ref, pres_ref, grad_ref, sems):
    copies = [
        pltpu.make_async_copy(grad_in, grad_ref, sems.at[0]),
        pltpu.make_async_copy(pen_in, pen_ref, sems.at[1]),
        pltpu.make_async_copy(pres_in, pres_ref, sems.at[2]),
    ]
    for copy in copies:
        copy.start()
    for copy in copies:
        copy.wait()


def per_device(n, lodf, limits, base_flow, first_ids, second_ids, counts):
    width, lines = lodf.shape
    firsts, cands = second_ids.shape
    vmem = pl.BlockSpec(memory_space=pltpu.VMEM)
    anywhere = pl.BlockSpec(memory_space=pl.ANY)
    penalty, pressure, grad = pl.pallas_call(
        functools.partial(kernel, n),
        out_shape=(
            pltpu.VMEM((firsts, cands), F32),
            pltpu.VMEM((1, width), F32),
            pltpu.VMEM((width, lines), BF16),
        ),
        in_specs=[anywhere] * 6,
        out_specs=(vmem, vmem, vmem),
        scratch_shapes=[
            pltpu.VMEM((n, 4 * firsts, cands), BF16),
            pltpu.VMEM((n, firsts, cands), F32),
            pltpu.VMEM((n, firsts, cands), F32),
            pltpu.VMEM((width, cands), F32),
            pltpu.VMEM((width, cands), F32),
            pltpu.VMEM((width, cands), F32),
            pltpu.VMEM((firsts, cands), F32),
            pltpu.VMEM((width, lines), BF16),
            pltpu.VMEM((width, width), BF16),
            pltpu.VMEM((1, width), jnp.int32),
            pltpu.VMEM((1, width), F32),
            pltpu.VMEM((firsts, cands), jnp.int32),
            pltpu.SMEM((firsts,), jnp.int32),
            pltpu.SMEM((firsts,), jnp.int32),
            pltpu.SemaphoreType.DMA((n,)),
            pltpu.SemaphoreType.DMA((n,)),
            pltpu.SemaphoreType.DMA((n,)),
            pltpu.SemaphoreType.DMA((n,)),
            pltpu.SemaphoreType.DMA((7,)),
        ],
        compiler_params=pltpu.CompilerParams(collective_id=0, has_side_effects=True),
        name="screen",
    )(first_ids, counts, lodf, limits.reshape(1, width), base_flow.reshape(1, width), second_ids)
    penalty, pressure, grad = pl.pallas_call(
        hand_out,
        out_shape=(
            jax.ShapeDtypeStruct((firsts, cands), F32),
            jax.ShapeDtypeStruct((1, width), F32),
            jax.ShapeDtypeStruct((width, lines), BF16),
        ),
        in_specs=[anywhere] * 3,
        out_specs=(anywhere,) * 3,
        scratch_shapes=[pltpu.SemaphoreType.DMA((3,))],
        compiler_params=pltpu.CompilerParams(vmem_limit_bytes=1 << 20),
        name="hand_out",
    )(penalty, pressure, grad)
    return penalty, pressure.reshape(width), grad


def solution(mesh):
    return jax.shard_map(
        functools.partial(per_device, mesh.shape["line"]),
        mesh=mesh,
        in_specs=(
            P("line", None),
            P("line"),
            P(("groups", "line")),
            P(("groups", "line")),
            P(("groups", "line"), None),
            P(("groups", "line")),
        ),
        out_specs=(P(("groups", "line"), None), P(("groups", "line")), P(("groups", "line"), None)),
        check_vma=False,
    )
```

```python
import functools

import jax
import jax.numpy as jnp
from jax import lax
from jax.experimental import pallas as pl
from jax.experimental.pallas import tpu as pltpu
from jax.sharding import PartitionSpec as P


F32 = jnp.float32
BF16 = jnp.bfloat16
MESH = pl.DeviceIdType.MESH


def split_bf16(x):
    hi = x.astype(BF16)
    return hi, (x - hi.astype(F32)).astype(BF16)


def partners(half, chip, s):
    if half & (half - 1):
        return lax.rem(chip + half - s, half), lax.rem(chip + s, half)
    other, bit = 0, 1
    while bit < half:
        other = other + bit * lax.rem(chip // bit + s // bit, 2)
        bit *= 2
    return other, other


def kernel(
    n,
    first_hbm,
    counts_hbm,
    lodf_hbm,
    limits_hbm,
    base_hbm,
    second_hbm,
    pen_ref,
    pres_ref,
    grad_ref,
    msgs,
    squares,
    landed,
    pres_acc,
    lower_ref,
    upper_ref,
    dead_ref,
    lodf_ref,
    square_ref,
    limits_ref,
    base_ref,
    second_ref,
    first_ref,
    counts_ref,
    send_sem,
    recv_sem,
    back_send_sem,
    back_recv_sem,
    load_sem,
):
    me = lax.axis_index("line")
    width = lodf_ref.shape[0]
    firsts, cands = second_ref.shape
    anchor = pl.multiple_of(me * width, width)
    half = n // 2
    chip, core = me // 2, lax.rem(me, 2)
    mate = 2 * chip + 1 - core

    barrier = pltpu.get_barrier_semaphore()

    def greet(t):
        pl.semaphore_signal(barrier, inc=1, device_id={"line": t}, device_id_type=MESH)

    for s in range(half - 1, 0, -1):
        there, _ = partners(half, chip, s)
        greet(2 * there + core)
        greet(2 * there + 1 - core)
    greet(mate)

    loads = [
        pltpu.make_async_copy(lodf_hbm.at[:, pl.ds(anchor, width)], square_ref, load_sem.at[0]),
        pltpu.make_async_copy(first_hbm, first_ref, load_sem.at[1]),
        pltpu.make_async_copy(counts_hbm, counts_ref, load_sem.at[2]),
        pltpu.make_async_copy(second_hbm, second_ref, load_sem.at[3]),
        pltpu.make_async_copy(base_hbm, base_ref, load_sem.at[4]),
        pltpu.make_async_copy(limits_hbm, limits_ref, load_sem.at[5]),
        pltpu.make_async_copy(lodf_hbm, lodf_ref, load_sem.at[6]),
    ]
    for load in loads:
        load.start()

    line_f = lax.broadcasted_iota(jnp.int32, (width, cands), 0).astype(F32)
    lane_f = lax.broadcasted_iota(jnp.int32, (width, width), 1).astype(F32)
    line_b = line_f.astype(BF16)
    slot_row = lax.broadcasted_iota(jnp.int32, (1, cands), 1)
    row_of = lax.broadcasted_iota(jnp.int32, (firsts, width), 0)
    lane_of = lax.broadcasted_iota(jnp.int32, (firsts, width), 1)
    for load in loads[:-1]:
        load.wait()

    base_t = jnp.transpose(jnp.broadcast_to(base_ref[...], (cands, width)))
    limit_t = 0.01 * jnp.transpose(jnp.broadcast_to(limits_ref[...].astype(F32), (cands, width)))
    lower_ref[...] = -limit_t - base_t
    upper_ref[...] = limit_t - base_t
    square = square_ref[...]
    second_f = (second_ref[...] - anchor).astype(F32)
    k1_rows, p_rows, q_rows, live_rows = [], [], [], []
    for j in range(firsts):
        k1 = jnp.full((1, cands), first_ref[j] - anchor, jnp.int32).astype(F32)
        k2 = second_f[j : j + 1, :]
        mask_one = line_f == k1
        mask_two = line_f == k2
        by_two = jnp.dot(square, mask_two.astype(F32).astype(BF16), preferred_element_type=F32)
        by_one = jnp.dot(square, mask_one.astype(F32).astype(BF16), preferred_element_type=F32)
        p_rows.append(jnp.sum(jnp.where(mask_one, by_two, 0.0), axis=0, keepdims=True))
        q_rows.append(jnp.sum(jnp.where(mask_two, by_one, 0.0), axis=0, keepdims=True))
        k1_rows.append(k1)
        live_rows.append((slot_row < counts_ref[j]).astype(F32))
    live = jnp.concatenate(live_rows, axis=0)
    base_rows = jnp.broadcast_to(base_ref[...], (firsts, width))
    turned = pltpu.roll(base_rows, width // 2, 1)
    halves = jnp.where(lax.rem(row_of, 2) == 0, base_rows, turned)
    halves_hi = halves.astype(BF16).astype(F32)
    base_parts = jnp.where(row_of < 2, halves_hi, halves - halves_hi)
    tail = jnp.where(lane_of < width // 2, base_parts, jnp.concatenate(k1_rows, axis=0))
    msgs[me] = jnp.concatenate(
        [
            jnp.where(live > 0.0, second_f, -1.0),
            jnp.concatenate(p_rows, axis=0),
            jnp.concatenate(q_rows, axis=0),
            tail,
        ],
        axis=0,
    ).astype(BF16)

    def out_copy(t, source):
        return pltpu.make_async_remote_copy(
            src_ref=msgs.at[source],
            dst_ref=msgs.at[source],
            send_sem=send_sem.at[t],
            recv_sem=recv_sem.at[source],
            device_id={"line": t},
            device_id_type=MESH,
        )

    def back_copy(t, source):
        return pltpu.make_async_remote_copy(
            src_ref=squares.at[t],
            dst_ref=landed.at[source],
            send_sem=back_send_sem.at[t],
            recv_sem=back_recv_sem.at[source],
            device_id={"line": t},
            device_id_type=MESH,
        )

    grad_scale = 2.0 / cands

    def add_piece(spread, weighted, hots):
        return spread + lax.dot_general(
            weighted, hots, (((1,), (1,)), ((), ())), preferred_element_type=F32
        )

    def tile(t, own, later=False):
        block = msgs[t].astype(F32)
        k2s = block[0:firsts]
        p = block[firsts : 2 * firsts]
        q = block[2 * firsts : 3 * firsts]
        tail = block[3 * firsts : 4 * firsts]
        k1s = jnp.broadcast_to(tail[:, width - 1 : width], (firsts, width))
        pair = tail[0:2] + tail[2:4]
        flow_row = jnp.where(
            lane_of < width // 2,
            jnp.broadcast_to(pair[0:1], (firsts, width)),
            pltpu.roll(jnp.broadcast_to(pair[1:2], (firsts, width)), width // 2, 1),
        )
        b1 = jnp.take_along_axis(flow_row, k1s.astype(jnp.int32), axis=1)
        b2 = jnp.take_along_axis(flow_row, jnp.maximum(k2s, 0.0).astype(jnp.int32), axis=1)
        alive = k2s >= 0.0
        det = 1.0 - p * q
        a1s = jnp.where(alive, (b1 + p * b2) / det, 0.0)
        a2s = jnp.where(alive, (b2 + q * b1) / det, 0.0)
        columns = lodf_ref[:, pl.ds(pl.multiple_of(t * width, width), width)]
        columns = jnp.concatenate([columns, columns], axis=1)
        a1_hi, a1_lo = split_bf16(a1s)
        a2_hi, a2_lo = split_bf16(a2s)
        k2_b, k1_b = k2s.astype(BF16), k1s.astype(BF16)
        zero_b = jnp.zeros((width, cands), BF16)
        one_b = jnp.ones((width, cands), BF16)
        spread = jnp.zeros((width, width), F32)
        first_sums = jnp.zeros((width, width), F32)
        pressure = jnp.zeros((width, cands), F32)
        square_rows, pieces = [], []
        for j0 in range(0, firsts, 2):
            hots, mixes = [], []
            for j in (j0, j0 + 1):
                row = slice(j, j + 1)
                at_two = line_b == jnp.broadcast_to(k2_b[row], (width, cands))
                at_one = line_b == jnp.broadcast_to(k1_b[row], (width, cands))

                hot = jnp.where(at_two, one_b, zero_b)

                def place(two, one):
                    two = jnp.broadcast_to(two, (width, cands))
                    one = jnp.broadcast_to(one, (width, cands))
                    return hot * two + jnp.where(at_one, one, zero_b)

                hots.append(hot)
                mixes.append(
                    jnp.concatenate(
                        [place(a2_hi[row], a1_hi[row]), place(a2_lo[row], a1_lo[row])], axis=0
                    )
                )
            mixed = jnp.dot(
                columns, jnp.concatenate(mixes, axis=1), preferred_element_type=F32
            )
            weighted = []
            for i, j in enumerate((j0, j0 + 1)):
                row = slice(j, j + 1)
                x = mixed[:, i * cands : (i + 1) * cands]
                e = x - jnp.minimum(jnp.maximum(x, lower_ref[...]), upper_ref[...])
                if own:
                    keep = (line_f != k2s[row]) & (line_f != k1s[row]) & (k2s[row] >= 0.0)
                    e = jnp.where(keep, e, 0.0)
                square_rows.append(jnp.sum(e * e, axis=0, keepdims=True))
                pressure = pressure + e
                weighted.append((e * a2s[row]).astype(BF16))
                one_sum = jnp.sum(e * a1s[row], axis=1, keepdims=True)
                first_sums = jnp.where(lane_f == float(j), one_sum, first_sums)
            pieces.append((jnp.concatenate(weighted, axis=1), jnp.concatenate(hots, axis=1)))
            if not later:
                spread = add_piece(spread, *pieces.pop())
        squares[t] = jnp.concatenate(square_rows, axis=0)

        def finish(spread):
            for piece in pieces:
                spread = add_piece(spread, *piece)
            hot_one = jnp.where(lane_of.astype(F32) == k1s, 1.0, 0.0)
            hot_one = jnp.concatenate([hot_one, jnp.zeros((width - firsts, width), F32)], axis=0)
            hot_one = hot_one.astype(BF16)
            sums_hi, sums_lo = split_bf16(first_sums)
            spread = spread + jnp.dot(
                jnp.concatenate([sums_hi, sums_lo], axis=1),
                jnp.concatenate([hot_one, hot_one], axis=0),
                preferred_element_type=F32,
            )
            grad_ref[:, pl.ds(pl.multiple_of(t * width, width), width)] = (
                spread * grad_scale
            ).astype(grad_ref.dtype)
            if own:
                pres_acc[...] = pressure
                dead_ref[...] = jnp.zeros_like(dead_ref)
            else:
                pres_acc[...] += pressure
                dead_ref[...] += jnp.where(k2s < 0.0, 1.0, 0.0)

        if later:
            return functools.partial(finish, spread)
        finish(spread)
        return None

    loads[-1].wait()
    starts_late = chip >= half - half // 2

    @pl.when(jnp.logical_not(starts_late))
    def _():
        tile(me, True)

    pl.semaphore_wait(barrier, n - 1)
    out_copy(mate, me).start()
    for s in range(half - 1, 0, -1):
        there, _ = partners(half, chip, s)
        out_copy(2 * there + core, me).start()
        out_copy(2 * there + 1 - core, me).start()

    @pl.when(starts_late)
    def _():
        tile(me, True)

    out_copy(mate, mate).wait_recv()
    tile(mate, False)
    back_copy(mate, me).start()

    def screen(steps, later=False):
        tiles = []
        for s in steps:
            _, there = partners(half, chip, s)
            tiles += [2 * there + core, 2 * there + 1 - core]
        for t in tiles:
            out_copy(t, t).wait_recv()
        finishes = [tile(t, False, later) for t in tiles]
        for t in tiles:
            back_copy(t, me).start()
        for finish in finishes:
            if later:
                finish()

    near = min(3, half - 1)
    order = [1, 2, 3, 7, 5, 4, 6] if half == 8 else list(range(1, half))
    if half <= 8:
        early = min(3, half - 2)
        steps = []
        for i, s in enumerate(order):
            if i == early:
                steps.append(jnp.where(chip == 0, s, chip))
            else:
                steps.append(jnp.where(chip == s, order[early], s))
        second = chip + 1 - 2 * lax.rem(chip, 2)
        for i in range(early + 2, len(steps)):
            moved = steps[i] == second
            steps[early + 1], steps[i] = (
                jnp.where(moved, steps[i], steps[early + 1]),
                jnp.where(moved, steps[early + 1], steps[i]),
            )
        for first, last in ((0, 1), (1, 3), (3, 5), (5, 7)):
            screen(steps[first:last], first >= early)
    else:

        @pl.loop(0, half - 1)
        def _(i):
            screen([jnp.where(i < near, i + 1, half - 1 + near - i)])

    n_dead = jnp.sum(dead_ref[...])
    resting = -jnp.minimum(jnp.maximum(0.0, lower_ref[...]), upper_ref[...])
    lines_sum = jnp.sum(jnp.transpose(pres_acc[...]), axis=0, keepdims=True)
    rest_row = jnp.transpose(resting)[0:1, :]
    pairs = n * firsts * cands
    pres_ref[...] = (lines_sum - n_dead * rest_row) * (2.0 / pairs)

    landed[me] = squares[me]
    alive_now = jnp.where(msgs[me].astype(F32)[0:firsts] >= 0.0, 1.0 / (n * width), 0.0)

    @pl.loop(1, n)
    def _(s):
        t = lax.rem(me + s, n)
        out_copy(t, me).wait_send()
        back_copy(t, me).wait_send()

    @pl.loop(1, n)
    def _(s):
        t = lax.rem(me + s, n)
        back_copy(t, t).wait_recv()

    pen_ref[...] = jnp.sum(landed[...], axis=0) * alive_now


def hand_out(pen_in, pres_in, grad_in, pen_ref, pres_ref, grad_ref, sems):
    copies = [
        pltpu.make_async_copy(grad_in, grad_ref, sems.at[0]),
        pltpu.make_async_copy(pen_in, pen_ref, sems.at[1]),
        pltpu.make_async_copy(pres_in, pres_ref, sems.at[2]),
    ]
    for copy in copies:
        copy.start()
    for copy in copies:
        copy.wait()


def per_device(n, lodf, limits, base_flow, first_ids, second_ids, counts):
    width, lines = lodf.shape
    firsts, cands = second_ids.shape
    vmem = pl.BlockSpec(memory_space=pltpu.VMEM)
    anywhere = pl.BlockSpec(memory_space=pl.ANY)
    penalty, pressure, grad = pl.pallas_call(
        functools.partial(kernel, n),
        out_shape=(
            pltpu.VMEM((firsts, cands), F32),
            pltpu.VMEM((1, width), F32),
            pltpu.VMEM((width, lines), BF16),
        ),
        in_specs=[anywhere] * 6,
        out_specs=(vmem, vmem, vmem),
        scratch_shapes=[
            pltpu.VMEM((n, 4 * firsts, cands), BF16),
            pltpu.VMEM((n, firsts, cands), F32),
            pltpu.VMEM((n, firsts, cands), F32),
            pltpu.VMEM((width, cands), F32),
            pltpu.VMEM((width, cands), F32),
            pltpu.VMEM((width, cands), F32),
            pltpu.VMEM((firsts, cands), F32),
            pltpu.VMEM((width, lines), BF16),
            pltpu.VMEM((width, width), BF16),
            pltpu.VMEM((1, width), jnp.int32),
            pltpu.VMEM((1, width), F32),
            pltpu.VMEM((firsts, cands), jnp.int32),
            pltpu.SMEM((firsts,), jnp.int32),
            pltpu.SMEM((firsts,), jnp.int32),
            pltpu.SemaphoreType.DMA((n,)),
            pltpu.SemaphoreType.DMA((n,)),
            pltpu.SemaphoreType.DMA((n,)),
            pltpu.SemaphoreType.DMA((n,)),
            pltpu.SemaphoreType.DMA((7,)),
        ],
        compiler_params=pltpu.CompilerParams(collective_id=0, has_side_effects=True),
        name="screen",
    )(first_ids, counts, lodf, limits.reshape(1, width), base_flow.reshape(1, width), second_ids)
    penalty, pressure, grad = pl.pallas_call(
        hand_out,
        out_shape=(
            jax.ShapeDtypeStruct((firsts, cands), F32),
            jax.ShapeDtypeStruct((1, width), F32),
            jax.ShapeDtypeStruct((width, lines), BF16),
        ),
        in_specs=[anywhere] * 3,
        out_specs=(anywhere,) * 3,
        scratch_shapes=[pltpu.SemaphoreType.DMA((3,))],
        compiler_params=pltpu.CompilerParams(vmem_limit_bytes=1 << 20),
        name="hand_out",
    )(penalty, pressure, grad)
    return penalty, pressure.reshape(width), grad


def solution(mesh):
    return jax.shard_map(
        functools.partial(per_device, mesh.shape["line"]),
        mesh=mesh,
        in_specs=(
            P("line", None),
            P("line"),
            P(("groups", "line")),
            P(("groups", "line")),
            P(("groups", "line"), None),
            P(("groups", "line")),
        ),
        out_specs=(P(("groups", "line"), None), P(("groups", "line")), P(("groups", "line"), None)),
        check_vma=False,
    )
```

```python
import functools

import jax
import jax.numpy as jnp
from jax import lax
from jax.experimental import pallas as pl
from jax.experimental.pallas import tpu as pltpu
from jax.sharding import PartitionSpec as P


F32 = jnp.float32
BF16 = jnp.bfloat16
MESH = pl.DeviceIdType.MESH


def split_bf16(x):
    hi = x.astype(BF16)
    return hi, (x - hi.astype(F32)).astype(BF16)


def partners(half, chip, s):
    if half & (half - 1):
        return lax.rem(chip + half - s, half), lax.rem(chip + s, half)
    other, bit = 0, 1
    while bit < half:
        other = other + bit * lax.rem(chip // bit + s // bit, 2)
        bit *= 2
    return other, other


def kernel(
    n,
    first_hbm,
    counts_hbm,
    lodf_hbm,
    limits_hbm,
    base_hbm,
    second_hbm,
    pen_ref,
    pres_ref,
    grad_ref,
    msgs,
    squares,
    landed,
    pres_acc,
    lower_ref,
    upper_ref,
    dead_ref,
    lodf_ref,
    square_ref,
    limits_ref,
    base_ref,
    second_ref,
    first_ref,
    counts_ref,
    send_sem,
    recv_sem,
    back_send_sem,
    back_recv_sem,
    load_sem,
):
    me = lax.axis_index("line")
    width = lodf_ref.shape[0]
    firsts, cands = second_ref.shape
    anchor = pl.multiple_of(me * width, width)
    half = n // 2
    chip, core = me // 2, lax.rem(me, 2)
    mate = 2 * chip + 1 - core

    barrier = pltpu.get_barrier_semaphore()

    def greet(t):
        pl.semaphore_signal(barrier, inc=1, device_id={"line": t}, device_id_type=MESH)

    for s in range(half - 1, 0, -1):
        there, _ = partners(half, chip, s)
        greet(2 * there + core)
        greet(2 * there + 1 - core)
    greet(mate)

    loads = [
        pltpu.make_async_copy(lodf_hbm.at[:, pl.ds(anchor, width)], square_ref, load_sem.at[0]),
        pltpu.make_async_copy(first_hbm, first_ref, load_sem.at[1]),
        pltpu.make_async_copy(counts_hbm, counts_ref, load_sem.at[2]),
        pltpu.make_async_copy(second_hbm, second_ref, load_sem.at[3]),
        pltpu.make_async_copy(base_hbm, base_ref, load_sem.at[4]),
        pltpu.make_async_copy(limits_hbm, limits_ref, load_sem.at[5]),
        pltpu.make_async_copy(lodf_hbm, lodf_ref, load_sem.at[6]),
    ]
    for load in loads:
        load.start()

    line_f = lax.broadcasted_iota(jnp.int32, (width, cands), 0).astype(F32)
    lane_f = lax.broadcasted_iota(jnp.int32, (width, width), 1).astype(F32)
    line_b = line_f.astype(BF16)
    slot_row = lax.broadcasted_iota(jnp.int32, (1, cands), 1)
    row_of = lax.broadcasted_iota(jnp.int32, (firsts, width), 0)
    lane_of = lax.broadcasted_iota(jnp.int32, (firsts, width), 1)
    for load in loads[:-1]:
        load.wait()

    base_t = jnp.transpose(jnp.broadcast_to(base_ref[...], (cands, width)))
    limit_t = 0.01 * jnp.transpose(jnp.broadcast_to(limits_ref[...].astype(F32), (cands, width)))
    lower_ref[...] = -limit_t - base_t
    upper_ref[...] = limit_t - base_t
    square = square_ref[...]
    second_f = (second_ref[...] - anchor).astype(F32)
    k1_rows, p_rows, q_rows, live_rows = [], [], [], []
    for j in range(firsts):
        k1 = jnp.full((1, cands), first_ref[j] - anchor, jnp.int32).astype(F32)
        k2 = second_f[j : j + 1, :]
        mask_one = line_f == k1
        mask_two = line_f == k2
        by_two = jnp.dot(square, mask_two.astype(F32).astype(BF16), preferred_element_type=F32)
        by_one = jnp.dot(square, mask_one.astype(F32).astype(BF16), preferred_element_type=F32)
        p_rows.append(jnp.sum(jnp.where(mask_one, by_two, 0.0), axis=0, keepdims=True))
        q_rows.append(jnp.sum(jnp.where(mask_two, by_one, 0.0), axis=0, keepdims=True))
        k1_rows.append(k1)
        live_rows.append((slot_row < counts_ref[j]).astype(F32))
    live = jnp.concatenate(live_rows, axis=0)
    base_rows = jnp.broadcast_to(base_ref[...], (firsts, width))
    turned = pltpu.roll(base_rows, width // 2, 1)
    halves = jnp.where(lax.rem(row_of, 2) == 0, base_rows, turned)
    halves_hi = halves.astype(BF16).astype(F32)
    base_parts = jnp.where(row_of < 2, halves_hi, halves - halves_hi)
    tail = jnp.where(lane_of < width // 2, base_parts, jnp.concatenate(k1_rows, axis=0))
    msgs[me] = jnp.concatenate(
        [
            jnp.where(live > 0.0, second_f, -1.0),
            jnp.concatenate(p_rows, axis=0),
            jnp.concatenate(q_rows, axis=0),
            tail,
        ],
        axis=0,
    ).astype(BF16)

    def out_copy(t, source):
        return pltpu.make_async_remote_copy(
            src_ref=msgs.at[source],
            dst_ref=msgs.at[source],
            send_sem=send_sem.at[t],
            recv_sem=recv_sem.at[source],
            device_id={"line": t},
            device_id_type=MESH,
        )

    def back_copy(t, source):
        return pltpu.make_async_remote_copy(
            src_ref=squares.at[t],
            dst_ref=landed.at[source],
            send_sem=back_send_sem.at[t],
            recv_sem=back_recv_sem.at[source],
            device_id={"line": t},
            device_id_type=MESH,
        )

    grad_scale = 2.0 / cands

    def add_piece(spread, weighted, hots):
        return spread + lax.dot_general(
            weighted, hots, (((1,), (1,)), ((), ())), preferred_element_type=F32
        )

    def tile(t, own, later=False):
        block = msgs[t].astype(F32)
        k2s = block[0:firsts]
        p = block[firsts : 2 * firsts]
        q = block[2 * firsts : 3 * firsts]
        tail = block[3 * firsts : 4 * firsts]
        k1s = jnp.broadcast_to(tail[:, width - 1 : width], (firsts, width))
        pair = tail[0:2] + tail[2:4]
        flow_row = jnp.where(
            lane_of < width // 2,
            jnp.broadcast_to(pair[0:1], (firsts, width)),
            pltpu.roll(jnp.broadcast_to(pair[1:2], (firsts, width)), width // 2, 1),
        )
        b1 = jnp.take_along_axis(flow_row, k1s.astype(jnp.int32), axis=1)
        b2 = jnp.take_along_axis(flow_row, jnp.maximum(k2s, 0.0).astype(jnp.int32), axis=1)
        alive = k2s >= 0.0
        det = 1.0 - p * q
        a1s = jnp.where(alive, (b1 + p * b2) / det, 0.0)
        a2s = jnp.where(alive, (b2 + q * b1) / det, 0.0)
        columns = lodf_ref[:, pl.ds(pl.multiple_of(t * width, width), width)]
        columns = jnp.concatenate([columns, columns], axis=1)
        a1_hi, a1_lo = split_bf16(a1s)
        a2_hi, a2_lo = split_bf16(a2s)
        k2_b, k1_b = k2s.astype(BF16), k1s.astype(BF16)
        zero_b = jnp.zeros((width, cands), BF16)
        one_b = jnp.ones((width, cands), BF16)
        spread = jnp.zeros((width, width), F32)
        first_sums = jnp.zeros((width, width), F32)
        pressure = jnp.zeros((width, cands), F32)
        square_rows, pieces = [], []
        for j0 in range(0, firsts, 2):
            hots, mixes = [], []
            for j in (j0, j0 + 1):
                row = slice(j, j + 1)
                at_two = line_b == jnp.broadcast_to(k2_b[row], (width, cands))
                at_one = line_b == jnp.broadcast_to(k1_b[row], (width, cands))

                hot = jnp.where(at_two, one_b, zero_b)

                def place(two, one):
                    two = jnp.broadcast_to(two, (width, cands))
                    one = jnp.broadcast_to(one, (width, cands))
                    return hot * two + jnp.where(at_one, one, zero_b)

                hots.append(hot)
                mixes.append(
                    jnp.concatenate(
                        [place(a2_hi[row], a1_hi[row]), place(a2_lo[row], a1_lo[row])], axis=0
                    )
                )
            mixed = jnp.dot(
                columns, jnp.concatenate(mixes, axis=1), preferred_element_type=F32
            )
            weighted = []
            for i, j in enumerate((j0, j0 + 1)):
                row = slice(j, j + 1)
                x = mixed[:, i * cands : (i + 1) * cands]
                e = x - jnp.minimum(jnp.maximum(x, lower_ref[...]), upper_ref[...])
                if own:
                    keep = (line_f != k2s[row]) & (line_f != k1s[row]) & (k2s[row] >= 0.0)
                    e = jnp.where(keep, e, 0.0)
                square_rows.append(jnp.sum(e * e, axis=0, keepdims=True))
                pressure = pressure + e
                weighted.append((e * a2s[row]).astype(BF16))
                one_sum = jnp.sum(e * a1s[row], axis=1, keepdims=True)
                first_sums = jnp.where(lane_f == float(j), one_sum, first_sums)
            pieces.append((jnp.concatenate(weighted, axis=1), jnp.concatenate(hots, axis=1)))
            if not later:
                spread = add_piece(spread, *pieces.pop())
        squares[t] = jnp.concatenate(square_rows, axis=0)

        def finish(spread):
            for piece in pieces:
                spread = add_piece(spread, *piece)
            hot_one = jnp.where(lane_of.astype(F32) == k1s, 1.0, 0.0)
            hot_one = jnp.concatenate([hot_one, jnp.zeros((width - firsts, width), F32)], axis=0)
            hot_one = hot_one.astype(BF16)
            sums_hi, sums_lo = split_bf16(first_sums)
            spread = spread + jnp.dot(
                jnp.concatenate([sums_hi, sums_lo], axis=1),
                jnp.concatenate([hot_one, hot_one], axis=0),
                preferred_element_type=F32,
            )
            grad_ref[:, pl.ds(pl.multiple_of(t * width, width), width)] = (
                spread * grad_scale
            ).astype(grad_ref.dtype)
            if own:
                pres_acc[...] = pressure
                dead_ref[...] = jnp.zeros_like(dead_ref)
            else:
                pres_acc[...] += pressure
                dead_ref[...] += jnp.where(k2s < 0.0, 1.0, 0.0)

        if later:
            return functools.partial(finish, spread)
        finish(spread)
        return None

    loads[-1].wait()
    starts_late = chip >= half - 2

    @pl.when(jnp.logical_not(starts_late))
    def _():
        tile(me, True)

    pl.semaphore_wait(barrier, n - 1)
    out_copy(mate, me).start()
    for s in range(half - 1, 0, -1):
        there, _ = partners(half, chip, s)
        out_copy(2 * there + core, me).start()
        out_copy(2 * there + 1 - core, me).start()

    @pl.when(starts_late)
    def _():
        tile(me, True)

    out_copy(mate, mate).wait_recv()
    tile(mate, False)
    back_copy(mate, me).start()

    def screen(steps, later=False):
        tiles = []
        for s in steps:
            _, there = partners(half, chip, s)
            tiles += [2 * there + core, 2 * there + 1 - core]
        for t in tiles:
            out_copy(t, t).wait_recv()
        finishes = [tile(t, False, later) for t in tiles]
        for t in tiles:
            back_copy(t, me).start()
        for finish in finishes:
            if later:
                finish()

    near = min(3, half - 1)
    order = [1, 2, 3, 7, 5, 4, 6] if half == 8 else list(range(1, half))
    if half <= 8:
        early = min(3, half - 2)
        steps = []
        for i, s in enumerate(order):
            if i == early:
                steps.append(jnp.where(chip == 0, s, chip))
            else:
                steps.append(jnp.where(chip == s, order[early], s))
        second = chip + 1 - 2 * lax.rem(chip, 2)
        for i in range(early + 2, len(steps)):
            moved = steps[i] == second
            steps[early + 1], steps[i] = (
                jnp.where(moved, steps[i], steps[early + 1]),
                jnp.where(moved, steps[early + 1], steps[i]),
            )
        for first, last in ((0, 1), (1, 3), (3, 4), (4, 7)):
            screen(steps[first:last], first >= early)
    else:

        @pl.loop(0, half - 1)
        def _(i):
            screen([jnp.where(i < near, i + 1, half - 1 + near - i)])

    n_dead = jnp.sum(dead_ref[...])
    resting = -jnp.minimum(jnp.maximum(0.0, lower_ref[...]), upper_ref[...])
    lines_sum = jnp.sum(jnp.transpose(pres_acc[...]), axis=0, keepdims=True)
    rest_row = jnp.transpose(resting)[0:1, :]
    pairs = n * firsts * cands
    pres_ref[...] = (lines_sum - n_dead * rest_row) * (2.0 / pairs)

    landed[me] = squares[me]
    alive_now = jnp.where(msgs[me].astype(F32)[0:firsts] >= 0.0, 1.0 / (n * width), 0.0)

    @pl.loop(1, n)
    def _(s):
        t = lax.rem(me + s, n)
        out_copy(t, me).wait_send()
        back_copy(t, me).wait_send()

    @pl.loop(1, n)
    def _(s):
        t = lax.rem(me + s, n)
        back_copy(t, t).wait_recv()

    pen_ref[...] = jnp.sum(landed[...], axis=0) * alive_now


def hand_out(pen_in, pres_in, grad_in, pen_ref, pres_ref, grad_ref, sems):
    copies = [
        pltpu.make_async_copy(grad_in, grad_ref, sems.at[0]),
        pltpu.make_async_copy(pen_in, pen_ref, sems.at[1]),
        pltpu.make_async_copy(pres_in, pres_ref, sems.at[2]),
    ]
    for copy in copies:
        copy.start()
    for copy in copies:
        copy.wait()


def per_device(n, lodf, limits, base_flow, first_ids, second_ids, counts):
    width, lines = lodf.shape
    firsts, cands = second_ids.shape
    vmem = pl.BlockSpec(memory_space=pltpu.VMEM)
    anywhere = pl.BlockSpec(memory_space=pl.ANY)
    penalty, pressure, grad = pl.pallas_call(
        functools.partial(kernel, n),
        out_shape=(
            pltpu.VMEM((firsts, cands), F32),
            pltpu.VMEM((1, width), F32),
            pltpu.VMEM((width, lines), BF16),
        ),
        in_specs=[anywhere] * 6,
        out_specs=(vmem, vmem, vmem),
        scratch_shapes=[
            pltpu.VMEM((n, 4 * firsts, cands), BF16),
            pltpu.VMEM((n, firsts, cands), F32),
            pltpu.VMEM((n, firsts, cands), F32),
            pltpu.VMEM((width, cands), F32),
            pltpu.VMEM((width, cands), F32),
            pltpu.VMEM((width, cands), F32),
            pltpu.VMEM((firsts, cands), F32),
            pltpu.VMEM((width, lines), BF16),
            pltpu.VMEM((width, width), BF16),
            pltpu.VMEM((1, width), jnp.int32),
            pltpu.VMEM((1, width), F32),
            pltpu.VMEM((firsts, cands), jnp.int32),
            pltpu.SMEM((firsts,), jnp.int32),
            pltpu.SMEM((firsts,), jnp.int32),
            pltpu.SemaphoreType.DMA((n,)),
            pltpu.SemaphoreType.DMA((n,)),
            pltpu.SemaphoreType.DMA((n,)),
            pltpu.SemaphoreType.DMA((n,)),
            pltpu.SemaphoreType.DMA((7,)),
        ],
        compiler_params=pltpu.CompilerParams(collective_id=0, has_side_effects=True),
        name="screen",
    )(first_ids, counts, lodf, limits.reshape(1, width), base_flow.reshape(1, width), second_ids)
    penalty, pressure, grad = pl.pallas_call(
        hand_out,
        out_shape=(
            jax.ShapeDtypeStruct((firsts, cands), F32),
            jax.ShapeDtypeStruct((1, width), F32),
            jax.ShapeDtypeStruct((width, lines), BF16),
        ),
        in_specs=[anywhere] * 3,
        out_specs=(anywhere,) * 3,
        scratch_shapes=[pltpu.SemaphoreType.DMA((3,))],
        compiler_params=pltpu.CompilerParams(vmem_limit_bytes=1 << 20),
        name="hand_out",
    )(penalty, pressure, grad)
    return penalty, pressure.reshape(width), grad


def solution(mesh):
    return jax.shard_map(
        functools.partial(per_device, mesh.shape["line"]),
        mesh=mesh,
        in_specs=(
            P("line", None),
            P("line"),
            P(("groups", "line")),
            P(("groups", "line")),
            P(("groups", "line"), None),
            P(("groups", "line")),
        ),
        out_specs=(P(("groups", "line"), None), P(("groups", "line")), P(("groups", "line"), None)),
        check_vma=False,
    )
```
